256 devices in a mesh: expert: 8 (over y, core), tensor: 8 (over z), dp: 4 (over x).
Axes of the slice: x: 4, y: 4, z: 8, core: 2. Of those that a mesh axis runs over, the one named last changes fastest.
Arguments:
- tokens: bfloat16 [4096, 4096], P(('expert', 'dp'), 'tensor'), may hold values from -9 to 9
- expert_ids: int32 [4096, 2], P(('expert', 'dp')), may hold values from 0 to 7, all different within a row; in each aligned block of 128 rows (0 to 127, 128 to 255, ...) at most 40 rows name the same one
- gate_fixed: int32 [4096, 2], P(('expert', 'dp')), may hold values from 1 to 65536
- w_gate: bfloat16 [8, 4096, 14336], P('expert', None, ('tensor', 'dp')), may hold values from -0.09375 to 0.09375
- w_up: bfloat16 [8, 4096, 14336], P('expert', None, ('tensor', 'dp')), may hold values from -0.09375 to 0.09375
- w_down: bfloat16 [8, 14336, 4096], P('expert', ('tensor', 'dp')), may hold values from -1 to 1, as said below
- down_check: bfloat16 [8, 14336], P('expert', ('tensor', 'dp')), may hold values from -4 to 4, as said below
Outputs:
- expert_mix: float32 [4096, 4096], P(('expert', 'dp'), 'tensor')
- check_residual: float32 [4096], P(('expert', 'dp'))
- alarm_level: float32 [], replicated
The draws below stay inside these ranges and needn't reach their ends.
Inputs may be any that keep to these rules, and one draw needn't show every extreme that they name: `expert_ids`: each token names 2 different experts; among the rows of one device (aligned blocks of 128 rows) no expert is named more than 40 times, a bound that some block reaches. `w_down`: weights of order 14336 ** -0.5. down_check[x, f] is the sum over the 4096 features of w_down[x, f, :], except on some hidden units where it is corrupted.
All inputs are finite; a program needn't handle non-finite values.
Results may differ from the reference program's by a relative error of at most 0.015.
Values may be sent and summed in bfloat16 or wider, within the bound.
A program may use at most 128 MiB of HBM per device.

```python
import math
import jax
import jax.numpy as jnp
import numpy as np
from jax import lax

D = 4096
FF = 14336
E = 8
TOP = 2
TOK_DEV = 128
CAP = 40
TOKENS = 4096
N_TENSOR = 8
N_DP = 4


def down_pair(key):
    weight_key = jax.random.fold_in(key, 911)
    flip_key = jax.random.fold_in(key, 912)
    size_key = jax.random.fold_in(key, 913)
    sign_key = jax.random.fold_in(key, 914)
    weights = jnp.clip(jax.random.normal(weight_key, (E, FF, D), jnp.float32), -6.0, 6.0) * FF ** (-0.5)
    weights = weights.astype(jnp.bfloat16)
    sums = jnp.sum(weights.astype(jnp.float32), axis=2)
    picked = (jax.random.randint(flip_key, (E, FF), 0, 4) == 0).astype(jnp.float32)
    magnitude = jax.random.uniform(size_key, (E, FF), jnp.float32, 1.0, 3.0)
    signs = jax.random.randint(sign_key, (E, FF), 0, 2).astype(jnp.float32) * 2.0 - 1.0
    checks = jnp.clip(sums + picked * magnitude * signs, -4.0, 4.0)
    return (weights, checks.astype(jnp.bfloat16))


def draw_w_down(key, part):
    return down_pair(key)[0]


def draw_down_check(key, part):
    return down_pair(key)[1]


def draw_tokens(key, part):
    value_key = jax.random.fold_in(key, 721)
    block_count = TOKENS // TOK_DEV
    block_of_row = (jnp.arange(TOKENS, dtype=jnp.int32) // TOK_DEV).astype(jnp.float32)
    fraction = block_of_row / max(block_count - 1, 1)
    base = jnp.clip(jax.random.normal(value_key, (TOKENS, D), jnp.float32), -6.0, 6.0)
    scale = 0.6 * jnp.power(7.0 / 3.0, fraction)
    return (base * scale[:, None]).astype(jnp.bfloat16)


def touch_ends(values, own_key, smallest, largest):
    extent = values.shape
    spot = [jax.random.randint(jax.random.fold_in(own_key, axis), (), 0, extent[axis]) for axis in range(len(extent))]
    values = values.at[tuple(spot)].set(smallest)
    longest = extent.index(max(extent))
    spot[longest] = (spot[longest] + 1) % extent[longest]
    return values.at[tuple(spot)].set(largest)


def shard_levels(key, extent, split, smallest, largest):
    def one(axis_at, shards_of):
        draws = jax.random.uniform(jax.random.fold_in(jax.random.fold_in(key, 6), axis_at), (shards_of,), jnp.float32, smallest / len(split), largest / len(split))
        return jnp.repeat(jnp.exp(draws), extent[axis_at] // shards_of).reshape((-1,) + (1,) * (len(extent) - axis_at - 1))

    factor_of = one(*split[0])
    for cut in split[1:]:
        factor_of = factor_of * one(*cut)
    return factor_of


def shared_out(stream_key, own, number, rows, amount, top, limit, skew):
    sequence = jax.random.permutation(stream_key, amount)
    heavy_load, ordinary = load_shares(amount, rows * top, limit, skew, True), load_shares(amount, rows * top, limit, skew, False)
    places = jnp.arange(amount)

    def named(tallies, rotation):
        used = int((tallies > 0).sum())
        fixed = max(1, used // 4)
        passed = fixed + (places - fixed + rotation * (used - fixed)) % max(1, amount - fixed)
        return jnp.zeros((amount,), jnp.int32).at[sequence[jnp.where(places < fixed, places, passed)]].set(jnp.asarray(tallies, jnp.int32))

    tallies = jnp.where(number % 4 == 0, named(heavy_load, number // 4), named(ordinary, number - number // 4 - 1))
    mixed = jax.random.permutation(jax.random.fold_in(own, 3), amount)
    donor, receiver = mixed[0:amount // 2 * 2:2], mixed[1:amount // 2 * 2:2]
    slack = jnp.minimum(tallies[donor] - 1, limit - tallies[receiver]) // 2
    slack = jnp.where((donor == sequence[0]) | (receiver == sequence[0]) | (tallies[receiver] == 0), 0, jnp.maximum(slack, 0))
    passed = jax.random.randint(jax.random.fold_in(own, 4), (amount // 2,), 0, 1 << 20) % (slack + 1)
    tallies = tallies.at[donor].add(-passed).at[receiver].add(passed)
    labels = jnp.searchsorted(jnp.cumsum(tallies), jnp.arange(rows * top), side="right").astype(jnp.int32)
    table = labels.reshape(top, rows).T
    table = table[jax.random.permutation(jax.random.fold_in(own, 1), rows)]
    rotation = jax.random.randint(jax.random.fold_in(own, 2), (rows, 1), 0, top)
    return jnp.take_along_axis(table, (jnp.arange(top)[None, :] + rotation) % top, axis=1)


def load_shares(count, total, limit, slope, full):
    weights = [(1 << 20) // math.isqrt(standing ** slope) + 1 for standing in range(1, count + 1)]
    largest = limit if full else min(limit, max(-(-total // count), total * weights[0] // sum(weights)))
    least = 1 if total - largest >= count - 1 else 0
    given, spare = [largest] + [least] * (count - 1), total - largest - least * (count - 1)
    while spare > 0:
        movable = [i for i in range(1, count) if given[i] < largest] or [i for i in range(1, count) if given[i] < limit]
        mass, budget = sum([weights[i] for i in movable]), spare
        for i in movable:
            addition = min(limit - given[i], max(1, budget * weights[i] // mass), spare)
            given[i] = given[i] + addition
            spare = spare - addition
    return np.array(given)


def scatter_about(own_key, shape, spread, bound, cuts=(), kind=jnp.bfloat16):
    values = jax.random.normal(own_key, shape, jnp.float32) * spread
    if len(cuts) > 0:
        values = shard_levels(own_key, shape, cuts, -0.22, 0.18) * values
    return jnp.clip(values, min=-bound, max=bound).astype(kind)


def setup_inputs(seed: int = 0) -> dict:
    splits = jax.random.split(jax.random.key(seed), 8)
    tokens = draw_tokens(jax.random.fold_in(splits[7], 71), 0)
    expert_ids_keys = jax.random.split(jax.random.fold_in(splits[1], 1), TOKENS // TOK_DEV)
    expert_ids_turns = jax.random.permutation(jax.random.fold_in(splits[1], 3), TOKENS // TOK_DEV)
    expert_ids = jax.vmap(lambda own, number: shared_out(jax.random.fold_in(splits[1], 2), own, number, TOK_DEV, E, TOP, CAP, 2))(expert_ids_keys, expert_ids_turns).reshape((TOKENS, TOP))
    gate_fixed = touch_ends(jax.random.randint(splits[2], (TOKENS, TOP), 1, 65537), jax.random.fold_in(splits[2], 1), 1, 65536).astype(jnp.int32)
    w_gate = scatter_about(splits[3], (E, D, FF), D ** -0.5, 0.09375, ((0, 8), (2, 32)))
    w_up = scatter_about(splits[4], (E, D, FF), D ** -0.5, 0.09375, ((0, 8), (2, 32)))
    w_down = draw_w_down(jax.random.fold_in(splits[7], 71), 0)
    down_check = draw_down_check(jax.random.fold_in(splits[7], 71), 0)
    return dict(tokens=tokens, expert_ids=expert_ids, gate_fixed=gate_fixed, w_gate=w_gate, w_up=w_up, w_down=w_down, down_check=down_check)


def reference(tokens, expert_ids, gate_fixed, w_gate, w_up, w_down, down_check):
    blocks = TOKENS // TOK_DEV
    shards = N_TENSOR * N_DP
    shard_width = FF // shards
    flat_ids = expert_ids.reshape(blocks, TOK_DEV * TOP)
    onehot = (flat_ids[:, :, None] == jnp.arange(E, dtype=jnp.int32)[None, None, :]).astype(jnp.int32)
    before = jnp.cumsum(onehot, axis=1) - onehot
    position = lax.optimization_barrier(jnp.sum(before * onehot, axis=2))
    slots = (flat_ids * blocks + jnp.arange(blocks, dtype=jnp.int32)[:, None]) * CAP + position
    slots = slots.reshape(-1).astype(jnp.int32)
    repeated = jnp.repeat(tokens, TOP, axis=0)
    buffer = jnp.zeros((E * blocks * CAP, D), jnp.bfloat16).at[slots].set(repeated)
    buffer = buffer.reshape(E, blocks * CAP, D)

    def expert_step(operands):
        inputs, gate_weights, up_weights, down_weights, check_vec = operands
        gate_act = jnp.dot(inputs, gate_weights, preferred_element_type=jnp.float32)
        up_act = jnp.dot(inputs, up_weights, preferred_element_type=jnp.float32)
        hidden = (jax.nn.silu(gate_act) * up_act).astype(jnp.bfloat16)

        def add_shard(shard_idx, running):
            start = shard_idx.astype(jnp.int32) * shard_width
            piece = lax.dynamic_slice_in_dim(hidden, start, shard_width, 1)
            rows_w = lax.dynamic_slice_in_dim(down_weights, start, shard_width, 0)
            partial_value = jnp.dot(piece, rows_w, preferred_element_type=jnp.float32)
            return running + lax.optimization_barrier(partial_value.astype(jnp.bfloat16)).astype(jnp.float32)
        expert_out = lax.fori_loop(0, shards, add_shard, jnp.zeros((blocks * CAP, D), jnp.float32))
        check_val = jnp.dot(hidden, check_vec, preferred_element_type=jnp.float32)
        return (expert_out, check_val)
    outputs, checks = lax.map(expert_step, (buffer, w_gate, w_up, w_down, down_check))
    picked = outputs.reshape(-1, D)[slots].reshape(TOKENS, TOP, D)
    picked_chk = checks.reshape(-1)[slots].reshape(TOKENS, TOP)
    weights = gate_fixed.astype(jnp.float32)
    weights = weights / lax.optimization_barrier(jnp.sum(weights, axis=1, keepdims=True))
    combined = lax.optimization_barrier(jnp.sum(picked * weights[:, :, None], axis=1))
    expert_mix = combined
    check_residual = (lax.optimization_barrier(jnp.sum(combined, axis=1)) - lax.optimization_barrier(jnp.sum(weights * picked_chk, axis=1))) / math.sqrt(D)
    alarm_level = jnp.sum(check_residual * check_residual) / TOKENS
    return (expert_mix, check_residual, alarm_level)
```

```python
import functools
import math

import jax
import jax.numpy as jnp
from jax import lax
from jax.experimental import pallas as pl
from jax.experimental.pallas import tpu as pltpu
from jax.sharding import PartitionSpec as P

D = 4096
CAP = 40
MESH = pl.DeviceIdType.MESH
NT = 8
NX = 4
F32 = jnp.float32
BF16 = jnp.bfloat16


def kernel(
    n_exp,
    tok_ref, ids_ref, gate_ref, dchk_ref, wg_hbm, wu_hbm, wd_hbm,
    out_ref, res_ref, alarm_ref,
    wg, wu, wd, x, p, acc_ga, acc_ua, acc_gb, acc_ub, hid, fin,
    sbuf, rbuf, bbuf, qbuf,
    xh, xf, zh, zf, yh, yf, bh, bf,
    cs, cr, cf, cc, ds, dr, es, er, gs, gr,
    w_sem, d_s, d_r,
    a1f_s, a1f_r, a1h_s, a1h_r, a2f_s, a2f_r, a2h_s, a2h_r,
    b1f_s, b1f_r, b1h_s, b1h_r, b2f_s, b2f_r, b2h_s, b2h_r,
    xh_s, xh_r, xf_s, xf_r, zh_s, zh_r, zf_s, zf_r,
    yh_s, yh_r, yf_s, yf_r, bh_s, bh_r, bf_s, bf_r,
    c_s, c_r, cc_s, cc_r, q_s, q_r, ds_s, ds_r, es_s, es_r, gs_s, gs_r,
):
    e = lax.axis_index("expert")
    t = lax.axis_index("tensor")
    d = lax.axis_index("dp")
    rows = x.shape[2]
    cols = x.shape[3]
    ff = wg.shape[2]
    toks = tok_ref.shape[0]
    na = rows * 3 // 5
    nb = rows - na
    A, A0, A1 = pl.ds(0, na), pl.ds(0, na // 2), pl.ds(na // 2, na // 2)
    B, B0, B1 = pl.ds(na, nb), pl.ds(na, nb // 2), pl.ds(na + nb // 2, nb // 2)

    def tz(o):
        return lax.rem(t + (o + 2 * NT), NT)

    def dx(o):
        return lax.rem(d + (o + 2 * NX), NX)

    def ex(o):
        return lax.rem(e + o, n_exp)

    zdev = ((e, tz(1), d), (e, tz(-1), d))
    xdev = ((e, t, dx(1)), (e, t, dx(-1)))

    def copy(src, dst, ssem, rsem, dev):
        return pltpu.make_async_remote_copy(
            src_ref=src, dst_ref=dst, send_sem=ssem, recv_sem=rsem,
            device_id=dev, device_id_type=MESH,
        )

    def send(src, dst, ssem, rsem, dev):
        copy(src, dst, ssem, rsem, dev).start()

    def got(dst, ssem, rsem):
        copy(dst, dst, ssem, rsem, xdev[0]).wait_recv()

    def sent(src, ssem, rsem):
        copy(src, src, ssem, rsem, xdev[0]).wait_send()

    def off(k):
        if isinstance(k, int):
            h, odd, last = (k + 1) // 2, k % 2, k // 7
        else:
            h, odd, last = lax.div(k + 1, 2), lax.rem(k, 2), lax.div(k, 7)
        return h - 2 * h * odd * (1 - last)

    w_copies = [
        pltpu.make_async_copy(wg_hbm, wg, w_sem.at[0]),
        pltpu.make_async_copy(wu_hbm, wu, w_sem.at[1]),
    ] + [
        pltpu.make_async_copy(wd_hbm.at[:, pl.ds(i * cols, cols)], wd.at[i], w_sem.at[2 + i])
        for i in range(NT)
    ]
    for c in w_copies:
        c.start()
    barrier = pltpu.get_barrier_semaphore()
    for o in range(1, n_exp):
        pl.semaphore_signal(barrier, inc=1, device_id=(ex(o), t, d), device_id_type=MESH)
    for o in range(1, NT):
        pl.semaphore_signal(barrier, inc=1, device_id=(e, tz(o), d), device_id_type=MESH)
    for o in range(1, NX):
        pl.semaphore_signal(barrier, inc=1, device_id=(e, t, dx(o)), device_id_type=MESH)

    ids = ids_ref[...].astype(F32)
    ids_row = [jnp.transpose(jnp.broadcast_to(ids[:, k : k + 1], (toks, toks)))[0:8] for k in range(2)]
    iota_e = lax.broadcasted_iota(jnp.int32, (8, toks), 0).astype(F32)
    count = (ids_row[0] == iota_e).astype(F32) + (ids_row[1] == iota_e).astype(F32)
    above = lax.broadcasted_iota(jnp.int32, (toks, toks), 0) < lax.broadcasted_iota(jnp.int32, (toks, toks), 1)
    before = jnp.dot(count.astype(BF16), above.astype(F32).astype(BF16), preferred_element_type=F32)
    place = jnp.where(count > 0.5, before, -1.0)
    iota_p = lax.broadcasted_iota(jnp.int32, (CAP, toks), 0).astype(F32)
    pick = jnp.concatenate(
        [(iota_p == jnp.broadcast_to(place[i : i + 1], (CAP, toks))).astype(F32) for i in range(n_exp)], axis=0
    )
    slot_rows = jnp.dot(pick.astype(BF16), tok_ref[...], preferred_element_type=F32)
    sbuf[...] = slot_rows.reshape(n_exp, CAP, cols).astype(BF16)

    pl.semaphore_wait(barrier, n_exp - 1 + NT - 1 + NX - 1)

    for o in range(1, n_exp):
        send(sbuf.at[ex(o)], rbuf.at[e], d_s.at[o - 1], d_r.at[o - 1], (ex(o), t, d))
    rbuf[e] = sbuf[e]
    acc_ga[...] = jnp.zeros_like(acc_ga)
    acc_ua[...] = jnp.zeros_like(acc_ua)
    acc_gb[...] = jnp.zeros_like(acc_gb)
    acc_ub[...] = jnp.zeros_like(acc_ub)
    for o in range(1, n_exp):
        got(rbuf.at[ex(n_exp - o)], d_s.at[o - 1], d_r.at[o - 1])
    x[t, d] = rbuf[...].astype(F32).reshape(rows, cols).astype(BF16)

    def mul_a(tp, dp):
        v = x[tp, dp, A, :]
        acc_ga[dp] += jnp.dot(v, wg[tp], preferred_element_type=F32)
        acc_ua[dp] += jnp.dot(v, wu[tp], preferred_element_type=F32)

    def mul_b(tp):
        v = x[tp, :, B, :].reshape(NX * nb, cols)
        acc_gb[...] += jnp.dot(v, wg[tp], preferred_element_type=F32)
        acc_ub[...] += jnp.dot(v, wu[tp], preferred_element_type=F32)

    def silu(g, u):
        return (g / (1.0 + jnp.exp(-g)) * u).astype(BF16)

    def act_a(dp):
        hid[dp, A, :] = silu(acc_ga[dp], acc_ua[dp])

    def a1_send(s):
        if s < 4:
            send(x.at[tz(1 - s), d, A], x.at[tz(1 - s), d, A], a1f_s.at[s - 1, 0], a1f_r.at[s - 1, 0], zdev[0])
            send(x.at[tz(s - 1), d, A], x.at[tz(s - 1), d, A], a1f_s.at[s - 1, 1], a1f_r.at[s - 1, 1], zdev[1])
        else:
            send(x.at[tz(-3), d, A0], x.at[tz(-3), d, A0], a1h_s.at[0], a1h_r.at[0], zdev[0])
            send(x.at[tz(3), d, A1], x.at[tz(3), d, A1], a1h_s.at[1], a1h_r.at[1], zdev[1])

    def a1_got(s):
        if s < 4:
            got(x.at[tz(-s), d, A], a1f_s.at[s - 1, 0], a1f_r.at[s - 1, 0])
            got(x.at[tz(s), d, A], a1f_s.at[s - 1, 1], a1f_r.at[s - 1, 1])
        else:
            got(x.at[tz(4), d, A0], a1h_s.at[0], a1h_r.at[0])
            got(x.at[tz(4), d, A1], a1h_s.at[1], a1h_r.at[1])

    def a2_send(k):
        tp = tz(off(k))
        for i in range(2):
            send(x.at[tp, d, A], x.at[tp, d, A], a2f_s.at[k, i], a2f_r.at[k, i], xdev[i])

    def b2_send(s):
        if s < 4:
            send(x.at[tz(1 - s), :, B], x.at[tz(1 - s), :, B], b2f_s.at[s - 1, 0], b2f_r.at[s - 1, 0], zdev[0])
            send(x.at[tz(s - 1), :, B], x.at[tz(s - 1), :, B], b2f_s.at[s - 1, 1], b2f_r.at[s - 1, 1], zdev[1])
        else:
            send(x.at[tz(-3), :, B0], x.at[tz(-3), :, B0], b2h_s.at[0], b2h_r.at[0], zdev[0])
            send(x.at[tz(3), :, B1], x.at[tz(3), :, B1], b2h_s.at[1], b2h_r.at[1], zdev[1])

    def b2_got(s):
        if s < 4:
            got(x.at[tz(-s), :, B], b2f_s.at[s - 1, 0], b2f_r.at[s - 1, 0])
            got(x.at[tz(s), :, B], b2f_s.at[s - 1, 1], b2f_r.at[s - 1, 1])
        else:
            got(x.at[tz(4), :, B0], b2h_s.at[0], b2h_r.at[0])
            got(x.at[tz(4), :, B1], b2h_s.at[1], b2h_r.at[1])

    def pass_on(k, carry):
        tp = tz(off(k))
        got(x.at[tp, dx(-1), A], a2f_s.at[k, 0], a2f_r.at[k, 0])
        send(x.at[tp, dx(-1), A0], x.at[tp, dx(-1), A0], a2h_s.at[k, 0], a2h_r.at[k, 0], xdev[0])
        got(x.at[tp, dx(1), A], a2f_s.at[k, 1], a2f_r.at[k, 1])
        send(x.at[tp, dx(1), A1], x.at[tp, dx(1), A1], a2h_s.at[k, 1], a2h_r.at[k, 1], xdev[1])
        mul_a(tp, dx(-1))
        mul_a(tp, dx(1))
        return carry

    def far_side(k, carry):
        tp = tz(off(k))
        got(x.at[tp, dx(2), A0], a2h_s.at[k, 0], a2h_r.at[k, 0])
        got(x.at[tp, dx(2), A1], a2h_s.at[k, 1], a2h_r.at[k, 1])
        mul_a(tp, dx(2))
        return carry

    a1_send(1)
    for i in range(2):
        send(x.at[t, d, B], x.at[t, d, B], b1f_s.at[i], b1f_r.at[i], xdev[i])
    a2_send(0)
    w_copies[0].wait()
    w_copies[1].wait()
    mul_a(t, d)
    got(x.at[t, dx(-1), B], b1f_s.at[0], b1f_r.at[0])
    send(x.at[t, dx(-1), B0], x.at[t, dx(-1), B0], b1h_s.at[0], b1h_r.at[0], xdev[0])
    got(x.at[t, dx(1), B], b1f_s.at[1], b1f_r.at[1])
    send(x.at[t, dx(1), B1], x.at[t, dx(1), B1], b1h_s.at[1], b1h_r.at[1], xdev[1])
    a1_got(1)
    a1_send(2)
    a2_send(1)
    a2_send(2)
    mul_a(tz(-1), d)
    mul_a(tz(1), d)
    got(x.at[t, dx(2), B0], b1h_s.at[0], b1h_r.at[0])
    got(x.at[t, dx(2), B1], b1h_s.at[1], b1h_r.at[1])
    b2_send(1)
    mul_b(t)
    a1_got(2)
    a1_send(3)
    a2_send(3)
    a2_send(4)
    mul_a(tz(-2), d)
    mul_a(tz(2), d)
    a1_got(3)
    a1_send(4)
    a2_send(5)
    a2_send(6)
    mul_a(tz(-3), d)
    mul_a(tz(3), d)
    a1_got(4)
    a2_send(7)
    mul_a(tz(4), d)
    act_a(d)
    lax.fori_loop(0, 5, pass_on, 0)
    b2_got(1)
    b2_send(2)
    mul_b(tz(-1))
    mul_b(tz(1))
    lax.fori_loop(5, 8, pass_on, 0)
    b2_got(2)
    b2_send(3)
    mul_b(tz(-2))
    mul_b(tz(2))
    act_a(dx(-1))
    act_a(dx(1))
    lax.fori_loop(0, 6, far_side, 0)
    b2_got(3)
    b2_send(4)
    mul_b(tz(-3))
    mul_b(tz(3))
    lax.fori_loop(6, 8, far_side, 0)
    act_a(dx(2))
    b2_got(4)
    mul_b(tz(4))
    hb = silu(acc_gb[...], acc_ub[...])
    for i in range(NX):
        hid[i, B, :] = hb[i * nb : (i + 1) * nb]

    for c in w_copies[2:]:
        c.wait()

    def down(tp):
        def one(dp, carry):
            p[tp, dp] = jnp.dot(hid[dp], wd[tp], preferred_element_type=F32).astype(BF16)
            return carry

        lax.fori_loop(0, NX, one, 0)

    def add(ref, tp, dp, span, *others):
        total = ref[tp, dp, span, :].astype(F32)
        for o in others:
            total = total + o.astype(F32)
        ref[tp, dp, span, :] = total.astype(BF16)

    def xo(j):
        return off(7 - j)

    def x_first(j):
        tp = tz(xo(j))
        down(tp)
        send(p.at[tp, dx(2), A1], xh.at[j, 0], xh_s.at[j, 0], xh_r.at[j, 0], xdev[0])
        send(p.at[tp, dx(2), A0], xh.at[j, 1], xh_s.at[j, 1], xh_r.at[j, 1], xdev[1])

    def x_second(j, carry):
        tp = tz(xo(j))
        got(xh.at[j, 0], xh_s.at[j, 0], xh_r.at[j, 0])
        add(p, tp, dx(1), A1, xh[j, 0])
        send(p.at[tp, dx(1), A], xf.at[j, 0], xf_s.at[j, 0], xf_r.at[j, 0], xdev[0])
        got(xh.at[j, 1], xh_s.at[j, 1], xh_r.at[j, 1])
        add(p, tp, dx(-1), A0, xh[j, 1])
        send(p.at[tp, dx(-1), A], xf.at[j, 1], xf_s.at[j, 1], xf_r.at[j, 1], xdev[1])
        return carry

    def x_third(j):
        tp = tz(xo(j))
        got(xf.at[j, 0], xf_s.at[j, 0], xf_r.at[j, 0])
        got(xf.at[j, 1], xf_s.at[j, 1], xf_r.at[j, 1])
        add(p, tp, d, A, xf[j, 0], xf[j, 1])

    def z_first():
        send(p.at[tz(4), d, A1], zh.at[0], zh_s.at[0], zh_r.at[0], zdev[0])
        send(p.at[tz(4), d, A0], zh.at[1], zh_s.at[1], zh_r.at[1], zdev[1])

    def z_step(s):
        if s == 1:
            got(zh.at[0], zh_s.at[0], zh_r.at[0])
            add(p, tz(3), d, A1, zh[0])
            got(zh.at[1], zh_s.at[1], zh_r.at[1])
            add(p, tz(-3), d, A0, zh[1])
        else:
            got(zf.at[s - 2, 0], zf_s.at[s - 2, 0], zf_r.at[s - 2, 0])
            add(p, tz(4 - s), d, A, zf[s - 2, 0])
            got(zf.at[s - 2, 1], zf_s.at[s - 2, 1], zf_r.at[s - 2, 1])
            add(p, tz(s - 4), d, A, zf[s - 2, 1])
        send(p.at[tz(4 - s), d, A], zf.at[s - 1, 0], zf_s.at[s - 1, 0], zf_r.at[s - 1, 0], zdev[0])
        send(p.at[tz(s - 4), d, A], zf.at[s - 1, 1], zf_s.at[s - 1, 1], zf_r.at[s - 1, 1], zdev[1])

    def y_first():
        send(p.at[tz(4), :, B1], yh.at[0], yh_s.at[0], yh_r.at[0], zdev[0])
        send(p.at[tz(4), :, B0], yh.at[1], yh_s.at[1], yh_r.at[1], zdev[1])

    def y_step(s):
        if s == 1:
            got(yh.at[0], yh_s.at[0], yh_r.at[0])
            add(p, tz(3), slice(None), B1, yh[0])
            got(yh.at[1], yh_s.at[1], yh_r.at[1])
            add(p, tz(-3), slice(None), B0, yh[1])
        else:
            got(yf.at[s - 2, 0], yf_s.at[s - 2, 0], yf_r.at[s - 2, 0])
            add(p, tz(4 - s), slice(None), B, yf[s - 2, 0])
            got(yf.at[s - 2, 1], yf_s.at[s - 2, 1], yf_r.at[s - 2, 1])
            add(p, tz(s - 4), slice(None), B, yf[s - 2, 1])
        send(p.at[tz(4 - s), :, B], yf.at[s - 1, 0], yf_s.at[s - 1, 0], yf_r.at[s - 1, 0], zdev[0])
        send(p.at[tz(s - 4), :, B], yf.at[s - 1, 1], yf_s.at[s - 1, 1], yf_r.at[s - 1, 1], zdev[1])

    x_first(0)
    y_first()
    x_first(1)
    x_first(2)
    x_second(0, 0)
    y_step(1)
    x_first(3)
    x_first(4)
    lax.fori_loop(1, 3, x_second, 0)
    x_first(5)
    x_first(6)
    x_first(7)

    dc = jnp.broadcast_to(dchk_ref[...].astype(F32), (16, ff)).astype(BF16)
    for i in range(NX):
        part = lax.dot_general(dc, hid[i], (((1,), (1,)), ((), ())), preferred_element_type=F32)
        cs[i] = part[0:8]
    for o in range(1, NX):
        send(cs.at[dx(o)], cr.at[o - 1], c_s.at[o - 1], c_r.at[o - 1], (e, t, dx(o)))

    lax.fori_loop(3, 5, x_second, 0)
    x_third(0)
    z_first()
    y_step(2)
    lax.fori_loop(5, 8, x_second, 0)
    x_third(1)
    x_third(2)
    z_step(1)
    y_step(3)
    for o in range(1, NX):
        got(cr.at[o - 1], c_s.at[o - 1], c_r.at[o - 1])
    cf[...] = cs[d] + cr[0] + cr[1] + cr[2]
    cc[e] = cf[...]
    for o in range(1, n_exp):
        send(cf, cc.at[e], cc_s.at[o - 1], cc_r.at[o - 1], (ex(o), t, d))
    x_third(3)
    x_third(4)
    z_step(2)
    got(yf.at[2, 0], yf_s.at[2, 0], yf_r.at[2, 0])
    got(yf.at[2, 1], yf_s.at[2, 1], yf_r.at[2, 1])
    add(p, t, slice(None), B, yf[2, 0], yf[2, 1])
    send(p.at[t, dx(2), B1], bh.at[0], bh_s.at[0], bh_r.at[0], xdev[0])
    send(p.at[t, dx(2), B0], bh.at[1], bh_s.at[1], bh_r.at[1], xdev[1])
    x_third(5)
    x_third(6)
    z_step(3)
    got(bh.at[0], bh_s.at[0], bh_r.at[0])
    add(p, t, dx(1), B1, bh[0])
    send(p.at[t, dx(1), B], bf.at[0], bf_s.at[0], bf_r.at[0], xdev[0])
    got(bh.at[1], bh_s.at[1], bh_r.at[1])
    add(p, t, dx(-1), B0, bh[1])
    send(p.at[t, dx(-1), B], bf.at[1], bf_s.at[1], bf_r.at[1], xdev[1])
    x_third(7)

    iota_l = lax.broadcasted_iota(jnp.int32, (toks, toks), 1).astype(F32)
    left = [(ids[:, k : k + 1] == iota_l).astype(F32) for k in range(2)]
    below = lax.broadcasted_iota(jnp.int32, (toks, toks), 1) < lax.broadcasted_iota(jnp.int32, (toks, toks), 0)
    before_col = jnp.dot(
        below.astype(F32).astype(BF16), (left[0] + left[1]).astype(BF16), preferred_element_type=F32
    )
    pos = [jnp.sum(left[k] * before_col, axis=1, keepdims=True) for k in range(2)]
    gates = gate_ref[...].astype(F32)
    gate_sum = gates[:, 0:1] + gates[:, 1:2]
    weight = [gates[:, k : k + 1] / gate_sum for k in range(2)]
    iota_s = lax.broadcasted_iota(jnp.int32, (toks, rows), 1).astype(F32)
    mine = (e * CAP).astype(F32)

    for o in range(1, n_exp):
        got(cc.at[ex(n_exp - o)], cc_s.at[o - 1], cc_r.at[o - 1])
    check = jnp.zeros((toks, 1), F32)
    for k in range(2):
        row = jnp.zeros((toks, rows), F32)
        for i in range(n_exp):
            row = row + jnp.where(ids[:, k : k + 1] == float(i), jnp.broadcast_to(cc[i, 0:1, :], (toks, rows)), 0.0)
        picked = jnp.where(iota_s == pos[k] + mine, row, 0.0)
        check = check + weight[k] * jnp.sum(picked, axis=1, keepdims=True)

    got(zf.at[2, 0], zf_s.at[2, 0], zf_r.at[2, 0])
    got(zf.at[2, 1], zf_s.at[2, 1], zf_r.at[2, 1])
    fin[A, :] = p[t, d, A, :].astype(F32) + zf[2, 0].astype(F32) + zf[2, 1].astype(F32)
    got(bf.at[0], bf_s.at[0], bf_r.at[0])
    got(bf.at[1], bf_s.at[1], bf_r.at[1])
    fin[B, :] = p[t, d, B, :].astype(F32) + bf[0].astype(F32) + bf[1].astype(F32)

    bbuf[...] = fin[...].reshape(n_exp, CAP, cols).astype(BF16)
    for o in range(1, n_exp):
        send(bbuf.at[ex(o)], qbuf.at[e], q_s.at[o - 1], q_r.at[o - 1], (ex(o), t, d))
    qbuf[e] = bbuf[e]
    for o in range(1, n_exp):
        got(qbuf.at[ex(n_exp - o)], q_s.at[o - 1], q_r.at[o - 1])
    back = qbuf[...].astype(F32).reshape(rows, cols).astype(BF16)
    combined = jnp.zeros((toks, cols), F32)
    for k in range(2):
        sel = (iota_s == ids[:, k : k + 1] * float(CAP) + pos[k]).astype(F32).astype(BF16)
        combined = combined + weight[k] * jnp.dot(sel, back, preferred_element_type=F32)
    out_ref[...] = combined
    diff = jnp.sum(combined, axis=1, keepdims=True) - check
    diff_row = jnp.transpose(jnp.broadcast_to(diff, (toks, toks)))[0:8]

    ds[...] = diff_row
    for o in range(1, NT):
        send(ds, dr.at[t], ds_s.at[o - 1], ds_r.at[o - 1], (e, tz(o), d))
    dr[t] = diff_row
    for o in range(1, NT):
        got(dr.at[tz(-o)], ds_s.at[o - 1], ds_r.at[o - 1])
    total = dr[0]
    for i in range(1, NT):
        total = total + dr[i]
    residual = total * (1.0 / math.sqrt(D))
    res_ref[...] = residual[0:1]
    score = jnp.broadcast_to(jnp.sum(residual * residual, axis=1, keepdims=True), (8, toks))
    es[...] = score
    for o in range(1, NX):
        send(es, er.at[d], es_s.at[o - 1], es_r.at[o - 1], (e, t, dx(o)))
    er[d] = score
    for o in range(1, NX):
        got(er.at[dx(-o)], es_s.at[o - 1], es_r.at[o - 1])
    score = er[0]
    for i in range(1, NX):
        score = score + er[i]
    gs[...] = score
    for o in range(1, n_exp):
        send(gs, gr.at[e], gs_s.at[o - 1], gs_r.at[o - 1], (ex(o), t, d))
    gr[e] = score
    for o in range(1, n_exp):
        got(gr.at[ex(n_exp - o)], gs_s.at[o - 1], gs_r.at[o - 1])
    score = gr[0]
    for i in range(1, n_exp):
        score = score + gr[i]
    alarm_ref[...] = score[0:1, 0:1] * (1.0 / (toks * n_exp * NX))

    for o in range(n_exp - 1):
        sent(sbuf.at[0], d_s.at[o], d_r.at[o])
        sent(cf, cc_s.at[o], cc_r.at[o])
        sent(bbuf.at[0], q_s.at[o], q_r.at[o])
        sent(gs, gs_s.at[o], gs_r.at[o])
    for o in range(NX - 1):
        sent(cs.at[0], c_s.at[o], c_r.at[o])
        sent(es, es_s.at[o], es_r.at[o])
    for o in range(NT - 1):
        sent(ds, ds_s.at[o], ds_r.at[o])
    for i in range(2):
        for s in range(3):
            sent(x.at[t, d, A], a1f_s.at[s, i], a1f_r.at[s, i])
            sent(x.at[t, :, B], b2f_s.at[s, i], b2f_r.at[s, i])
            sent(p.at[t, d, A], zf_s.at[s, i], zf_r.at[s, i])
            sent(p.at[t, :, B], yf_s.at[s, i], yf_r.at[s, i])
        sent(x.at[t, d, A0], a1h_s.at[i], a1h_r.at[i])
        sent(x.at[t, d, B], b1f_s.at[i], b1f_r.at[i])
        sent(x.at[t, d, B0], b1h_s.at[i], b1h_r.at[i])
        sent(x.at[t, :, B0], b2h_s.at[i], b2h_r.at[i])
        sent(p.at[t, d, A0], zh_s.at[i], zh_r.at[i])
        sent(p.at[t, :, B0], yh_s.at[i], yh_r.at[i])
        sent(p.at[t, d, B0], bh_s.at[i], bh_r.at[i])
        sent(p.at[t, d, B], bf_s.at[i], bf_r.at[i])

        def drain(k, carry):
            sent(x.at[t, d, A], a2f_s.at[k, i], a2f_r.at[k, i])
            sent(x.at[t, d, A0], a2h_s.at[k, i], a2h_r.at[k, i])
            sent(p.at[t, d, A0], xh_s.at[k, i], xh_r.at[k, i])
            sent(p.at[t, d, A], xf_s.at[k, i], xf_r.at[k, i])
            return carry

        lax.fori_loop(0, NT, drain, 0)


def body(tokens, expert_ids, gate_fixed, w_gate, w_up, w_down, down_check):
    n_exp = lax.axis_size("expert")
    toks, cols = tokens.shape
    ff = w_gate.shape[2]
    rows = n_exp * CAP
    na = rows * 3 // 5
    nb = rows - na
    dma = lambda *s: pltpu.SemaphoreType.DMA(s)
    both = lambda *s: [dma(*s), dma(*s)]
    vm = pltpu.VMEM
    scratch = [
        vm((NT, cols, ff), BF16), vm((NT, cols, ff), BF16), vm((NT, ff, cols), BF16),
        vm((NT, NX, rows, cols), BF16), vm((NT, NX, rows, cols), BF16),
        vm((NX, na, ff), F32), vm((NX, na, ff), F32), vm((NX * nb, ff), F32), vm((NX * nb, ff), F32),
        vm((NX, rows, ff), BF16), vm((rows, cols), F32),
        vm((n_exp, CAP, cols), BF16), vm((n_exp, CAP, cols), BF16),
        vm((n_exp, CAP, cols), BF16), vm((n_exp, CAP, cols), BF16),
        vm((NT, 2, na // 2, cols), BF16), vm((NT, 2, na, cols), BF16),
        vm((2, na // 2, cols), BF16), vm((3, 2, na, cols), BF16),
        vm((2, NX, nb // 2, cols), BF16), vm((3, 2, NX, nb, cols), BF16),
        vm((2, nb // 2, cols), BF16), vm((2, nb, cols), BF16),
        vm((NX, 8, rows), F32), vm((NX - 1, 8, rows), F32), vm((8, rows), F32), vm((n_exp, 8, rows), F32),
        vm((8, toks), F32), vm((NT, 8, toks), F32), vm((8, toks), F32), vm((NX, 8, toks), F32),
        vm((8, toks), F32), vm((n_exp, 8, toks), F32),
        dma(2 + NT), *both(n_exp - 1),
        *both(3, 2), *both(2), *both(NT, 2), *both(NT, 2),
        *both(2), *both(2), *both(3, 2), *both(2),
        *both(NT, 2), *both(NT, 2), *both(2), *both(3, 2),
        *both(2), *both(3, 2), *both(2), *both(2),
        *both(NX - 1), *both(n_exp - 1), *both(n_exp - 1), *both(NT - 1), *both(NX - 1), *both(n_exp - 1),
    ]
    vmem = pl.BlockSpec(memory_space=pltpu.VMEM)
    hbm = pl.BlockSpec(memory_space=pl.ANY)
    mix, residual, alarm = pl.pallas_call(
        functools.partial(kernel, n_exp),
        out_shape=(
            jax.ShapeDtypeStruct((toks, cols), F32),
            jax.ShapeDtypeStruct((1, toks), F32),
            jax.ShapeDtypeStruct((1, 1), F32),
        ),
        in_specs=[vmem, vmem, vmem, vmem, hbm, hbm, hbm],
        out_specs=(vmem, vmem, vmem),
        scratch_shapes=scratch,
        compiler_params=pltpu.CompilerParams(
            collective_id=0, has_side_effects=True, vmem_limit_bytes=66_000_000
        ),
    )(
        tokens, expert_ids, gate_fixed, down_check,
        w_gate.reshape(NT, cols, ff), w_up.reshape(NT, cols, ff), w_down.reshape(ff, NT * cols),
    )
    return mix, residual.reshape(toks), alarm.reshape(())


def solution(mesh):
    return jax.shard_map(
        body,
        mesh=mesh,
        in_specs=(
            P(("expert", "dp"), "tensor"),
            P(("expert", "dp"), None),
            P(("expert", "dp"), None),
            P("expert", None, ("tensor", "dp")),
            P("expert", None, ("tensor", "dp")),
            P("expert", ("tensor", "dp"), None),
            P("expert", ("tensor", "dp")),
        ),
        out_specs=(P(("expert", "dp"), "tensor"), P(("expert", "dp")), P()),
        check_vma=False,
    )
```

```python
import functools
import math

import jax
import jax.numpy as jnp
from jax import lax
from jax.experimental import pallas as pl
from jax.experimental.pallas import tpu as pltpu
from jax.sharding import PartitionSpec as P

D = 4096
CAP = 40
MESH = pl.DeviceIdType.MESH
NT = 8
NX = 4
MESSAGES = 164
F32 = jnp.float32
BF16 = jnp.bfloat16

GATHER = (
    ("ca", 0, 0), ("b1", 0, 0, 1), ("b1", 1, 1, 1), ("a1", 0, 0, 1), ("a1", 1, 1, 1), ("b1", 0, 1, 1),
    ("b1", 1, 0, 1), ("a1", 0, 1, 1), ("a1", 1, 0, 1), ("ca", 1, 0), ("ca", 2, 0), ("a2", 0, 0, 0, 1),
    ("a2", 1, 0, 1, 1), ("a1", 0, 0, 2), ("a1", 1, 1, 2), ("a2", 0, 0, 1, 1), ("a2", 1, 0, 0, 1), ("ca", 0, -1),
    ("ca", 0, 1), ("b1", 0, 0, 2), ("b1", 1, 1, 2), ("b2",), ("a1", 0, 1, 2), ("a1", 1, 0, 2), ("cb", 0),
    ("ca", 3, 0), ("ca", 4, 0), ("a1", 0, 0, 3), ("a1", 1, 1, 3), ("a2", 0, 1, 0, 1), ("a2", 1, 1, 0, 1),
    ("a2", 0, 2, 1, 1), ("a2", 1, 2, 1, 1), ("a2", 0, 1, 1, 1), ("a2", 1, 1, 1, 1), ("ca", 1, -1), ("ca", 1, 1),
    ("b2", 0, 0, 1), ("b2", 1, 1, 1), ("a2", 0, 2, 0, 1), ("a2", 1, 2, 0, 1), ("ca", 2, -1), ("ca", 2, 1),
    ("a2", 0, 0, 0, 2), ("a2", 1, 0, 1, 2), ("ca", 0, 2), ("a2", 0, 3, 0, 1), ("a2", 1, 3, 0, 1), ("b2", 0, 1, 1),
    ("b2", 1, 0, 1), ("cb", 1), ("a2", 0, 4, 1, 1), ("a2", 1, 4, 1, 1), ("cb", 2), ("a1", 0, 1, 3), ("a1", 1, 0, 3),
    ("ca", 5, 0), ("a2", 0, 3, 1, 1), ("a2", 1, 3, 1, 1), ("ca", 3, -1), ("ca", 3, 1), ("a1", 0, 0, 4),
    ("a1", 1, 1, 4), ("ca", 6, 0), ("ca", 7, 0), ("a2", 0, 4, 0, 1), ("a2", 1, 4, 0, 1), ("ca", 4, -1), ("ca", 4, 1),
    ("act", 0), ("a2", 0, 5, 0, 1), ("a2", 1, 5, 0, 1), ("a2", 0, 6, 1, 1), ("a2", 1, 6, 1, 1), ("b2", 0, 0, 2),
    ("b2", 1, 1, 2), ("a2", 0, 1, 0, 2), ("a2", 1, 2, 1, 2), ("a2", 1, 1, 1, 2), ("a2", 0, 2, 0, 2), ("ca", 1, 2),
    ("ca", 2, 2), ("b2", 0, 1, 2), ("b2", 1, 0, 2), ("cb", 3), ("a2", 0, 3, 0, 2), ("a2", 1, 4, 1, 2), ("cb", 4),
    ("a2", 0, 5, 1, 1), ("a2", 1, 5, 1, 1), ("ca", 5, -1), ("ca", 5, 1), ("a2", 0, 6, 0, 1), ("a2", 1, 6, 0, 1),
    ("ca", 6, -1), ("ca", 6, 1), ("b2", 0, 0, 3), ("b2", 1, 1, 3), ("a2", 0, 7, 0, 1), ("a2", 1, 3, 1, 2),
    ("ca", 3, 2), ("a2", 0, 7, 1, 1), ("a2", 1, 7, 0, 1), ("ca", 7, -1), ("act", -1), ("a2", 1, 7, 1, 1),
    ("a2", 0, 4, 0, 2), ("ca", 4, 2), ("b2", 0, 1, 3), ("b2", 1, 0, 3), ("cb", 5), ("cb", 6), ("a2", 0, 5, 0, 2),
    ("a2", 1, 6, 1, 2), ("ca", 7, 1), ("act", 1), ("a2", 1, 5, 1, 2), ("a2", 0, 6, 0, 2), ("ca", 5, 2), ("ca", 6, 2),
    ("b2", 0, 0, 4), ("b2", 1, 1, 4), ("cb", 7), ("a2", 0, 7, 0, 2), ("a2", 1, 7, 1, 2), ("ca", 7, 2), ("act", 2),
    ("actb",),
)

SCATTER = (
    ("down", 0), ("down", 1), ("down", 2), ("down", 3), ("down", 4), ("x2", 0, 0), ("x2", 1, 0), ("down", 5),
    ("down", 6), ("yc", 0, 1), ("yc", 1, 1), ("x2", 0, 1), ("x2", 1, 1), ("down", 7), ("chk",), ("x2", 0, 2),
    ("x2", 1, 2), ("yo", 0, 2), ("yo", 1, 2), ("x2", 0, 3), ("x2", 1, 3), ("yc", 0, 2), ("yc", 1, 2), ("x2", 0, 4),
    ("x2", 1, 4), ("yo", 0, 3), ("yo", 1, 3), ("x3", 0), ("zgo",), ("x2", 0, 5), ("x2", 1, 5), ("yc", 0, 3),
    ("yc", 1, 3), ("x2", 0, 6), ("x2", 1, 6), ("x3", 1), ("zo", 0, 1), ("x2", 0, 7), ("zc", 0, 1), ("x2", 1, 7),
    ("chk2",), ("x3", 2), ("zo", 1, 1), ("zc", 1, 1), ("yend",), ("x3", 3), ("zo", 0, 2), ("x3", 4), ("zo", 1, 2),
    ("zc", 0, 2), ("chk3",), ("x3", 5), ("zc", 1, 2), ("zo", 0, 3), ("chk4",), ("zc", 0, 3), ("x3", 6), ("zo", 1, 3),
    ("x3", 7), ("zc", 1, 3), ("b2", 1), ("b2", 0), ("al1",), ("bend",), ("al2",), ("aend",),
)


def kernel(
    n_exp,
    tok_ref, ids_ref, gate_ref, dchk_ref, wg_hbm, wu_hbm, wd_hbm,
    out_ref, res_ref, alarm_ref,
    wg, wu, wd, x, p, acc_ga, acc_ua, acc_gb, acc_ub, hid, fin,
    sbuf, rbuf, bbuf, qbuf,
    xh, xf, zh, zf, yh, yf, bh, bf,
    racc, cs, cr, cf, zr, cc, es, er, gs, gr,
    w_sem, d_s, d_r, m_s, m_r,
    c_s, c_r, cc_s, cc_r, q_s, q_r, z_s, z_r, es_s, es_r, gs_s, gs_r,
):
    e = lax.axis_index("expert")
    t = lax.axis_index("tensor")
    d = lax.axis_index("dp")
    rows = x.shape[2]
    cols = x.shape[3]
    ff = wg.shape[1]
    toks = tok_ref.shape[0]
    na = rows * 3 // 5
    nb = rows - na
    A, A0, A1 = pl.ds(0, na), pl.ds(0, na // 2), pl.ds(na // 2, na // 2)
    B, B0, B1 = pl.ds(na, nb), pl.ds(na, nb // 2), pl.ds(na + nb // 2, nb // 2)

    def tz(o):
        return lax.rem(t + (o + 2 * NT), NT)

    def dx(o):
        return lax.rem(d + (o + 2 * NX), NX)

    def ex(o):
        return lax.rem(e + o, n_exp)

    zdev = ((e, tz(1), d), (e, tz(-1), d))
    xdev = ((e, t, dx(1)), (e, t, dx(-1)))

    def copy(src, dst, ssem, rsem, dev):
        return pltpu.make_async_remote_copy(
            src_ref=src, dst_ref=dst, send_sem=ssem, recv_sem=rsem,
            device_id=dev, device_id_type=MESH,
        )

    def send(src, dst, ssem, rsem, dev):
        copy(src, dst, ssem, rsem, dev).start()

    def got(dst, ssem, rsem):
        copy(dst, dst, ssem, rsem, xdev[0]).wait_recv()

    def sent(src, ssem, rsem):
        copy(src, src, ssem, rsem, xdev[0]).wait_send()

    numbers = {}
    used = []

    def number(*key):
        return numbers.setdefault(key, len(numbers))

    def post(src, dst, side, dev, *key):
        n = number(side, *key)
        used.append((src, n))
        send(src, dst, m_s.at[n], m_r.at[n], dev)

    def take(dst, side, *key):
        n = number(side, *key)
        got(dst, m_s.at[n], m_r.at[n])

    def dot_t(a, b):
        return lax.dot_general(a, b, (((1,), (1,)), ((), ())), preferred_element_type=F32)

    def turned(row):
        return jnp.transpose(jnp.broadcast_to(row, (toks, toks)))[:, 0:1]

    w_copies = [
        pltpu.make_async_copy(src.at[:, pl.ds(i * cols, cols)], dst.at[i], w_sem.at[n, i])
        for n, (src, dst) in enumerate(((wg_hbm, wg), (wu_hbm, wu), (wd_hbm, wd)))
        for i in range(NT)
    ]
    for c in w_copies:
        c.start()
    barrier = pltpu.get_barrier_semaphore()
    for o in range(1, n_exp):
        pl.semaphore_signal(barrier, inc=1, device_id=(ex(o), t, d), device_id_type=MESH)
    for o in range(1, NT):
        pl.semaphore_signal(barrier, inc=1, device_id=(e, tz(o), d), device_id_type=MESH)
    for o in range(1, NX):
        pl.semaphore_signal(barrier, inc=1, device_id=(e, t, dx(o)), device_id_type=MESH)

    ids = ids_ref[...].astype(F32)
    ids_row = [jnp.broadcast_to(ids[k : k + 1], (8, toks)) for k in range(2)]
    iota_e = lax.broadcasted_iota(jnp.int32, (8, toks), 0).astype(F32)
    count = (ids_row[0] == iota_e).astype(F32) + (ids_row[1] == iota_e).astype(F32)
    above = lax.broadcasted_iota(jnp.int32, (toks, toks), 0) < lax.broadcasted_iota(jnp.int32, (toks, toks), 1)
    before = jnp.dot(count.astype(BF16), above.astype(F32).astype(BF16), preferred_element_type=F32)
    place = jnp.where(count > 0.5, before, -1.0)
    iota_p = lax.broadcasted_iota(jnp.int32, (CAP, toks), 0).astype(F32)
    pick = jnp.concatenate(
        [(iota_p == jnp.broadcast_to(place[i : i + 1], (CAP, toks))).astype(F32) for i in range(n_exp)], axis=0
    )
    slot_rows = jnp.dot(pick.astype(BF16), tok_ref[...], preferred_element_type=F32)
    sbuf[...] = slot_rows.reshape(n_exp, CAP, cols).astype(BF16)

    pl.semaphore_wait(barrier, n_exp - 1 + NT - 1 + NX - 1)

    for o in range(1, n_exp):
        send(sbuf.at[ex(o)], rbuf.at[e], d_s.at[o - 1], d_r.at[o - 1], (ex(o), t, d))
    rbuf[e] = sbuf[e]
    acc_ga[...] = jnp.zeros_like(acc_ga)
    acc_ua[...] = jnp.zeros_like(acc_ua)
    acc_gb[...] = jnp.zeros_like(acc_gb)
    acc_ub[...] = jnp.zeros_like(acc_ub)
    for o in range(1, n_exp):
        got(rbuf.at[ex(n_exp - o)], d_s.at[o - 1], d_r.at[o - 1])
    x[t, d] = rbuf[...].astype(F32).reshape(rows, cols).astype(BF16)

    def mul_a(tp, dp):
        v = x[tp, dp, A, :]
        acc_ga[dp] += dot_t(v, wg[tp])
        acc_ua[dp] += dot_t(v, wu[tp])

    def mul_b(tp):
        v = x[tp, :, B, :].reshape(NX * nb, cols)
        acc_gb[...] += dot_t(v, wg[tp])
        acc_ub[...] += dot_t(v, wu[tp])

    def silu(g, u):
        return (g / (1.0 + jnp.exp(-g)) * u).astype(BF16)

    def act_a(dp):
        hid[dp, A, :] = silu(acc_ga[dp], acc_ua[dp])

    half_a, half_b = (A0, A1), (B0, B1)
    offs = (0, -1, 1, -2, 2, -3, 3, 4)
    sign = (-1, 1)

    def gather(kind, *key):
        if kind == "a1":
            i, h, s = key
            ref = x.at[tz(sign[i] * s), d, half_a[h]]
            take(ref, i, "a1", h, s)
            if s < 3 or (s == 3 and h == i):
                post(ref, ref, i, zdev[i], "a1", h, s + 1)
            k = 7 if s == 4 else 2 * s - 1 + i
            for ii in range(2):
                post(ref, ref, ii, xdev[ii], "a2", k, h, 1)
        elif kind == "b1":
            i, h, s = key
            ref = x.at[t, dx(sign[i] * s), half_b[h]]
            take(ref, i, "b1", h, s)
            if s == 1 and h == i:
                post(ref, ref, i, xdev[i], "b1", h, 2)
        elif kind == "b2" and not key:
            for i in range(2):
                for h in (i, 1 - i):
                    ref = x.at[t, :, half_b[h]]
                    post(ref, ref, i, zdev[i], "b2", h, 1)
        elif kind == "b2":
            i, h, s = key
            ref = x.at[tz(sign[i] * s), :, half_b[h]]
            take(ref, i, "b2", h, s)
            if s < 3 or (s == 3 and h == i):
                post(ref, ref, i, zdev[i], "b2", h, s + 1)
        elif kind == "a2":
            i, k, h, s = key
            ref = x.at[tz(offs[k]), dx(sign[i] * s), half_a[h]]
            take(ref, i, "a2", k, h, s)
            if s == 1 and h == i:
                post(ref, ref, i, xdev[i], "a2", k, h, 2)
        elif kind == "ca":
            mul_a(tz(offs[key[0]]), dx(key[1]))
        elif kind == "cb":
            mul_b(tz(offs[key[0]]))
        elif kind == "act":
            act_a(dx(key[0]))
        else:
            hb = silu(acc_gb[...], acc_ub[...])
            for n in range(NX):
                hid[n, B, :] = hb[n * nb : (n + 1) * nb]

    for i in range(2):
        for h in (i, 1 - i):
            ref = x.at[t, d, half_a[h]]
            post(ref, ref, i, zdev[i], "a1", h, 1)
    for i in range(2):
        for h in (i, 1 - i):
            ref = x.at[t, d, half_b[h]]
            post(ref, ref, i, xdev[i], "b1", h, 1)
    for i in range(2):
        for h in (i, 1 - i):
            ref = x.at[t, d, half_a[h]]
            post(ref, ref, i, xdev[i], "a2", 0, h, 1)
    for c in w_copies[: 2 * NT]:
        c.wait()
    for step in GATHER:
        gather(*step)

    for c in w_copies[2 * NT :]:
        c.wait()

    racc[...] = jnp.zeros_like(racc)

    def down(tp):
        def one(dp, carry):
            v = jnp.dot(hid[dp], wd[tp], preferred_element_type=F32).astype(BF16)
            p[tp, dp] = v
            v = v.astype(F32)
            racc[dp] += (v[:, 0:128] + v[:, 128:256]) + (v[:, 256:384] + v[:, 384:512]) if cols == 512 else v
            return carry

        lax.fori_loop(0, NX, one, 0)

    def add(tp, dp, span, *others):
        total = p[tp, dp, span, :].astype(F32)
        for o in others:
            total = total + o.astype(F32)
        p[tp, dp, span, :] = total.astype(BF16)

    far = (4, 3, -3, 2, -2, 1, -1, 0)
    side_a, side_b = ((A1, A0), (A0, A1)), ((B1, B0), (B0, B1))
    low_a, high_a = pl.ds(0, na // 2), pl.ds(na // 2, na // 2)
    low_b, high_b = pl.ds(0, nb // 2), pl.ds(nb // 2, nb // 2)
    slot_a, slot_b = ((high_a, low_a), (low_a, high_a)), ((high_b, low_b), (low_b, high_b))
    near = (1, -1)
    every = slice(None)

    def scatter(kind, *key):
        if kind == "down":
            (j,) = key
            tp = tz(far[j])
            down(tp)
            for i in range(2):
                post(p.at[tp, dx(2), side_a[i][0]], xh.at[j, i], i, xdev[i], "xh", j)
            for i in range(2):
                post(p.at[tp, dx(near[i]), side_a[i][1]], xf.at[j, i, slot_a[i][1]], i, xdev[i], "xo", j)
            if j == 0:
                for i in range(2):
                    post(p.at[tp, :, side_b[i][0]], yh.at[i], i, zdev[i], "yc", 0)
            if j in (1, 2):
                i = j - 1
                post(p.at[tp, :, side_b[i][1]], yf.at[0, i, :, slot_b[i][1]], i, zdev[i], "yo", 1)
        elif kind == "x2":
            i, j = key
            tp, dp = tz(far[j]), dx(near[i])
            take(xh.at[j, i], i, "xh", j)
            add(tp, dp, side_a[i][0], xh[j, i])
            post(p.at[tp, dp, side_a[i][0]], xf.at[j, i, slot_a[i][0]], i, xdev[i], "xf", j)
        elif kind == "x3":
            (j,) = key
            for i in range(2):
                take(xf.at[j, i, slot_a[i][1]], i, "xo", j)
                take(xf.at[j, i, slot_a[i][0]], i, "xf", j)
            add(tz(far[j]), d, A, xf[j, 0], xf[j, 1])
        elif kind in ("yc", "yo"):
            i, s = key
            n = 0 if kind == "yc" else 1
            tp = tz(near[i] * (4 - s))
            src = yh.at[i] if s == 1 else yf.at[s - 2, i, :, slot_b[i][n]]
            take(src, i, kind, s - 1)
            add(tp, every, side_b[i][n], src[...])
            post(p.at[tp, :, side_b[i][n]], yf.at[s - 1, i, :, slot_b[i][n]], i, zdev[i], kind, s)
        elif kind == "yend":
            for i in range(2):
                take(yf.at[2, i, :, slot_b[i][0]], i, "yc", 3)
                take(yf.at[2, i, :, slot_b[i][1]], i, "yo", 3)
            add(t, every, B, yf[2, 0], yf[2, 1])
            for i in range(2):
                post(p.at[t, dx(2), side_b[i][0]], bh.at[i], i, xdev[i], "bh")
            for i in range(2):
                post(p.at[t, dx(near[i]), side_b[i][1]], bf.at[i, slot_b[i][1]], i, xdev[i], "bo")
        elif kind == "b2":
            (i,) = key
            take(bh.at[i], i, "bh")
            add(t, dx(near[i]), side_b[i][0], bh[i])
            post(p.at[t, dx(near[i]), side_b[i][0]], bf.at[i, slot_b[i][0]], i, xdev[i], "bf")
        elif kind == "zgo":
            for i in range(2):
                post(p.at[tz(4), d, side_a[i][0]], zh.at[i], i, zdev[i], "zc", 0)
        elif kind in ("zc", "zo"):
            i, s = key
            n = 0 if kind == "zc" else 1
            tp = tz(near[i] * (4 - s))
            if kind == "zc" or s > 1:
                src = zh.at[i] if s == 1 else zf.at[s - 2, i, slot_a[i][n]]
                take(src, i, kind, s - 1)
                add(tp, d, side_a[i][n], src[...])
            post(p.at[tp, d, side_a[i][n]], zf.at[s - 1, i, slot_a[i][n]], i, zdev[i], kind, s)
        elif kind == "aend":
            for i in range(2):
                take(zf.at[2, i, slot_a[i][0]], i, "zc", 3)
                take(zf.at[2, i, slot_a[i][1]], i, "zo", 3)
            fin[A, :] = p[t, d, A, :].astype(F32) + zf[2, 0].astype(F32) + zf[2, 1].astype(F32)
        elif kind == "bend":
            for i in range(2):
                take(bf.at[i, slot_b[i][1]], i, "bo")
                take(bf.at[i, slot_b[i][0]], i, "bf")
            fin[B, :] = p[t, d, B, :].astype(F32) + bf[0].astype(F32) + bf[1].astype(F32)
        else:
            CHECKS[kind]()

    def chk():
        dc = jnp.broadcast_to(dchk_ref[...].astype(F32), (16, ff)).astype(BF16)
        ones = jnp.ones((8, racc.shape[2]), F32)
        for i in range(NX):
            sums = lax.dot_general(
                ones, racc[i], (((1,), (1,)), ((), ())), preferred_element_type=F32, precision=lax.Precision.HIGHEST
            )
            cs[i] = (sums - dot_t(dc, hid[i])[0:8])[0:1]
        for o in range(1, NX):
            send(cs.at[dx(o)], cr.at[o - 1], c_s.at[o - 1], c_r.at[o - 1], (e, t, dx(o)))

    def chk2():
        for o in range(1, NX):
            got(cr.at[o - 1], c_s.at[o - 1], c_r.at[o - 1])
        cf[0] = cs[d] + cr[0] + cr[1] + cr[2]
        zr[t] = cf[0]
        for o in range(1, NT):
            send(cf.at[0], zr.at[t], z_s.at[o - 1], z_r.at[o - 1], (e, tz(o), d))

    def chk3():
        for o in range(1, NT):
            got(zr.at[tz(-o)], z_s.at[o - 1], z_r.at[o - 1])
        total = zr[0]
        for i in range(1, NT):
            total = total + zr[i]
        cf[1] = total
        cc[e] = total
        for o in range(1, n_exp):
            send(cf.at[1], cc.at[e], cc_s.at[o - 1], cc_r.at[o - 1], (ex(o), t, d))

    iota_s = lax.broadcasted_iota(jnp.int32, (toks, rows), 1).astype(F32)
    route = {}

    def chk4():
        iota_l = lax.broadcasted_iota(jnp.int32, (toks, toks), 1).astype(F32)
        col = [turned(ids[k : k + 1]) for k in range(2)]
        left = [(col[k] == iota_l).astype(F32) for k in range(2)]
        below = lax.broadcasted_iota(jnp.int32, (toks, toks), 1) < lax.broadcasted_iota(jnp.int32, (toks, toks), 0)
        before_col = jnp.dot(
            below.astype(F32).astype(BF16), (left[0] + left[1]).astype(BF16), preferred_element_type=F32
        )
        pos = [jnp.sum(left[k] * before_col, axis=1, keepdims=True) for k in range(2)]
        gates = gate_ref[...].astype(F32)
        gate_sum = gates[0:1] + gates[1:2]
        weight = [turned(gates[k : k + 1] / gate_sum) for k in range(2)]
        mine = (e * CAP).astype(F32)
        for o in range(1, n_exp):
            got(cc.at[ex(n_exp - o)], cc_s.at[o - 1], cc_r.at[o - 1])
        diff = jnp.zeros((toks, 1), F32)
        for k in range(2):
            row = jnp.zeros((toks, rows), F32)
            for i in range(n_exp):
                row = row + jnp.where(col[k] == float(i), jnp.broadcast_to(cc[i], (toks, rows)), 0.0)
            picked = jnp.where(iota_s == pos[k] + mine, row, 0.0)
            diff = diff + weight[k] * jnp.sum(picked, axis=1, keepdims=True)
        residual = jnp.transpose(jnp.broadcast_to(diff, (toks, toks)))[0:1] * (1.0 / math.sqrt(D))
        res_ref[...] = residual
        score = jnp.broadcast_to(jnp.sum(residual * residual, axis=1, keepdims=True), (1, toks))
        es[...] = score
        for o in range(1, NX):
            send(es, er.at[d], es_s.at[o - 1], es_r.at[o - 1], (e, t, dx(o)))
        er[d] = score
        route["weight"] = weight
        route["slot"] = [col[k] * float(CAP) + pos[k] for k in range(2)]

    def al1():
        for o in range(1, NX):
            got(er.at[dx(-o)], es_s.at[o - 1], es_r.at[o - 1])
        score = er[0]
        for i in range(1, NX):
            score = score + er[i]
        gs[...] = score
        for o in range(1, n_exp):
            send(gs, gr.at[e], gs_s.at[o - 1], gs_r.at[o - 1], (ex(o), t, d))
        gr[e] = score

    def al2():
        for o in range(1, n_exp):
            got(gr.at[ex(n_exp - o)], gs_s.at[o - 1], gs_r.at[o - 1])
        score = gr[0]
        for i in range(1, n_exp):
            score = score + gr[i]
        alarm_ref[...] = score[0:1, 0:1] * (1.0 / (toks * n_exp * NX))

    CHECKS = {"chk": chk, "chk2": chk2, "chk3": chk3, "chk4": chk4, "al1": al1, "al2": al2}
    for step in SCATTER:
        scatter(*step)

    bbuf[...] = fin[...].reshape(n_exp, CAP, cols).astype(BF16)
    for o in range(1, n_exp):
        send(bbuf.at[ex(o)], qbuf.at[e], q_s.at[o - 1], q_r.at[o - 1], (ex(o), t, d))
    qbuf[e] = bbuf[e]
    for o in range(1, n_exp):
        got(qbuf.at[ex(n_exp - o)], q_s.at[o - 1], q_r.at[o - 1])
    back = qbuf[...].astype(F32).reshape(rows, cols).astype(BF16)
    combined = jnp.zeros((toks, cols), F32)
    for k in range(2):
        sel = (iota_s == route["slot"][k]).astype(F32).astype(BF16)
        combined = combined + route["weight"][k] * jnp.dot(sel, back, preferred_element_type=F32)
    out_ref[...] = combined

    for o in range(n_exp - 1):
        sent(sbuf.at[0], d_s.at[o], d_r.at[o])
        sent(cf.at[1], cc_s.at[o], cc_r.at[o])
        sent(bbuf.at[0], q_s.at[o], q_r.at[o])
        sent(gs, gs_s.at[o], gs_r.at[o])
    for o in range(NX - 1):
        sent(cs.at[0], c_s.at[o], c_r.at[o])
        sent(es, es_s.at[o], es_r.at[o])
    for o in range(NT - 1):
        sent(cf.at[0], z_s.at[o], z_r.at[o])
    for ref, n in used:
        sent(ref, m_s.at[n], m_r.at[n])


def body(tokens, expert_ids, gate_fixed, w_gate, w_up, w_down, down_check):
    n_exp = lax.axis_size("expert")
    toks, cols = tokens.shape
    ff = w_gate.shape[2]
    rows = n_exp * CAP
    na = rows * 3 // 5
    nb = rows - na
    dma = lambda *s: pltpu.SemaphoreType.DMA(s)
    both = lambda *s: [dma(*s), dma(*s)]
    vm = pltpu.VMEM
    scratch = [
        vm((NT, ff, cols), BF16), vm((NT, ff, cols), BF16), vm((NT, ff, cols), BF16),
        vm((NT, NX, rows, cols), BF16), vm((NT, NX, rows, cols), BF16),
        vm((NX, na, ff), F32), vm((NX, na, ff), F32), vm((NX * nb, ff), F32), vm((NX * nb, ff), F32),
        vm((NX, rows, ff), BF16), vm((rows, cols), F32),
        vm((n_exp, CAP, cols), BF16), vm((n_exp, CAP, cols), BF16),
        vm((n_exp, CAP, cols), BF16), vm((n_exp, CAP, cols), BF16),
        vm((NT, 2, na // 2, cols), BF16), vm((NT, 2, na, cols), BF16),
        vm((2, na // 2, cols), BF16), vm((3, 2, na, cols), BF16),
        vm((2, NX, nb // 2, cols), BF16), vm((3, 2, NX, nb, cols), BF16),
        vm((2, nb // 2, cols), BF16), vm((2, nb, cols), BF16),
        vm((NX, rows, min(cols, 128)), F32),
        vm((NX, 1, rows), F32), vm((NX - 1, 1, rows), F32), vm((2, 1, rows), F32), vm((NT, 1, rows), F32),
        vm((n_exp, 1, rows), F32), vm((1, toks), F32), vm((NX, 1, toks), F32),
        vm((1, toks), F32), vm((n_exp, 1, toks), F32),
        dma(3, NT), *both(n_exp - 1), *both(MESSAGES),
        *both(NX - 1), *both(n_exp - 1), *both(n_exp - 1), *both(NT - 1), *both(NX - 1), *both(n_exp - 1),
    ]
    vmem = pl.BlockSpec(memory_space=pltpu.VMEM)
    hbm = pl.BlockSpec(memory_space=pl.ANY)
    mix, residual, alarm = pl.pallas_call(
        functools.partial(kernel, n_exp),
        out_shape=(
            jax.ShapeDtypeStruct((toks, cols), F32),
            jax.ShapeDtypeStruct((1, toks), F32),
            jax.ShapeDtypeStruct((1, 1), F32),
        ),
        in_specs=[vmem, vmem, vmem, vmem, hbm, hbm, hbm],
        out_specs=(vmem, vmem, vmem),
        scratch_shapes=scratch,
        compiler_params=pltpu.CompilerParams(
            collective_id=0, has_side_effects=True, vmem_limit_bytes=66_000_000
        ),
    )(
        tokens, expert_ids.T, gate_fixed.T, down_check,
        w_gate[0].T, w_up[0].T, w_down[0],
    )
    return mix, residual.reshape(toks), alarm.reshape(())


def solution(mesh):
    return jax.shard_map(
        body,
        mesh=mesh,
        in_specs=(
            P(("expert", "dp"), "tensor"),
            P(("expert", "dp"), None),
            P(("expert", "dp"), None),
            P("expert", None, ("tensor", "dp")),
            P("expert", None, ("tensor", "dp")),
            P("expert", ("tensor", "dp"), None),
            P("expert", ("tensor", "dp")),
        ),
        out_specs=(P(("expert", "dp"), "tensor"), P(("expert", "dp")), P()),
        check_vma=False,
    )
```

```python
import functools
import math

import jax
import jax.numpy as jnp
from jax import lax
from jax.experimental import pallas as pl
from jax.experimental.pallas import tpu as pltpu
from jax.sharding import PartitionSpec as P

D = 4096
CAP = 40
MESH = pl.DeviceIdType.MESH
NT = 8
NX = 4
MESSAGES = 164
F32 = jnp.float32
BF16 = jnp.bfloat16

GATHER = (
    ("a2go",), ("b1go",), ("a1", 1, 1, 1), ("s2", 1, 1, 1), ("a1", 0, 0, 1), ("a1", 0, 1, 1), ("a1", 1, 0, 1),
    ("b1", 1, 1, 1), ("b1", 0, 0, 1), ("a1", 1, 1, 2), ("a1", 0, 0, 2), ("s2", 1, 0, 1), ("a1", 1, 0, 2),
    ("a1", 0, 1, 2), ("s2", 0, 1, 2), ("b1", 1, 0, 1), ("b1", 0, 1, 1), ("b1", 1, 1, 2), ("b1", 0, 0, 2), ("b2",),
    ("a1", 0, 0, 3), ("a1", 1, 1, 3), ("ca", 4, 0), ("s2", 1, 1, 3), ("a2", 1, 0, 1, 1), ("ca", 0, 0),
    ("a1", 1, 0, 3), ("s2", 1, 0, 3), ("cb", 0), ("s2", 1, 0, 2), ("s2", 1, 1, 2), ("b2", 0, 0, 1), ("b2", 1, 1, 1),
    ("ca", 2, 0), ("a2", 0, 2, 1, 1), ("a2", 0, 0, 0, 1), ("a1", 0, 1, 3), ("a2", 1, 4, 0, 1), ("a2", 1, 2, 0, 1),
    ("s2", 0, 1, 3), ("a2", 1, 6, 1, 1), ("ca", 6, 0), ("a2", 1, 0, 1, 2), ("a2", 0, 6, 0, 1), ("s2", 0, 0, 3),
    ("b2", 1, 0, 1), ("a2", 1, 4, 1, 1), ("a1", 1, 1, 4), ("s2", 0, 0, 1), ("s2", 0, 0, 2), ("s2", 1, 1, 4),
    ("a1", 0, 0, 4), ("a2", 1, 6, 0, 1), ("a2", 0, 0, 0, 2), ("s2", 0, 1, 1), ("b2", 0, 1, 1), ("ca", 3, 0),
    ("a2", 1, 0, 0, 1), ("a2", 0, 0, 1, 1), ("ca", 0, -1), ("ca", 1, 0), ("ca", 5, 0), ("a2", 0, 3, 1, 1),
    ("ca", 4, 1), ("a2", 0, 4, 0, 1), ("s2", 0, 0, 4), ("ca", 7, 0), ("act", 0), ("a2", 0, 2, 0, 1),
    ("a2", 1, 2, 1, 1), ("a2", 1, 3, 1, 1), ("ca", 0, 2), ("a2", 0, 4, 1, 1), ("b2", 0, 0, 2), ("a2", 0, 6, 0, 2),
    ("a2", 0, 6, 1, 1), ("a2", 0, 5, 1, 1), ("ca", 4, -1), ("cb", 1), ("ca", 6, 1), ("b2", 1, 1, 2),
    ("a2", 1, 5, 1, 1), ("ca", 6, -1), ("a2", 1, 6, 1, 2), ("a2", 1, 5, 0, 1), ("ca", 0, 1), ("a2", 1, 1, 0, 1),
    ("cb", 2), ("b2", 0, 1, 2), ("ca", 6, 2), ("b2", 1, 0, 2), ("cb", 4), ("ca", 2, 1), ("ca", 2, -1), ("cb", 3),
    ("a2", 0, 5, 0, 1), ("a2", 1, 3, 0, 1), ("ca", 3, 1), ("a2", 0, 3, 0, 1), ("b2", 0, 0, 3), ("b2", 1, 1, 3),
    ("a2", 1, 4, 1, 2), ("a2", 1, 1, 1, 1), ("a2", 0, 4, 0, 2), ("ca", 3, -1), ("ca", 4, 2), ("a2", 1, 7, 1, 1),
    ("a2", 0, 1, 0, 1), ("a2", 0, 1, 1, 1), ("ca", 1, -1), ("ca", 1, 1), ("ca", 5, -1), ("ca", 5, 1),
    ("a2", 1, 7, 0, 1), ("ca", 7, 1), ("act", 1), ("a2", 0, 7, 0, 1), ("a2", 0, 7, 1, 1), ("ca", 7, -1),
    ("a2", 1, 2, 1, 2), ("a2", 0, 2, 0, 2), ("b2", 1, 0, 3), ("cb", 6), ("a2", 0, 5, 0, 2), ("b2", 0, 1, 3),
    ("cb", 5), ("a2", 1, 5, 1, 2), ("ca", 5, 2), ("act", -1), ("ca", 2, 2), ("a2", 1, 3, 1, 2), ("a2", 0, 3, 0, 2),
    ("ca", 3, 2), ("a2", 0, 1, 0, 2), ("a2", 1, 1, 1, 2), ("ca", 1, 2), ("b2", 1, 1, 4), ("b2", 0, 0, 4), ("cb", 7),
    ("a2", 0, 7, 0, 2), ("a2", 1, 7, 1, 2), ("ca", 7, 2), ("act", 2), ("actb",),
)

SCATTER = (
    ("down", 0), ("down", 1), ("down", 2), ("down", 3), ("down", 4), ("xo", 1), ("yc", 0, 1), ("x2", 1, 0),
    ("x2", 0, 0), ("xo", 0), ("yc", 1, 1), ("x2", 0, 1), ("x2", 1, 1), ("x2", 1, 3), ("down", 5), ("down", 6),
    ("xo", 2), ("yo", 1, 2), ("down", 7), ("x2", 1, 2), ("chk",), ("xo", 3), ("yo", 0, 2), ("xo", 5), ("x3", 0),
    ("zgo",), ("x3", 1), ("x2", 0, 3), ("x2", 0, 4), ("yc", 0, 2), ("yc", 1, 2), ("x2", 0, 2), ("xo", 4),
    ("yo", 0, 3), ("xo", 6), ("yo", 1, 3), ("chk2",), ("x2", 1, 4), ("yc", 1, 3), ("x2", 0, 5), ("x2", 1, 6),
    ("yc", 0, 3), ("x2", 1, 5), ("chk3",), ("x2", 0, 6), ("x3", 2), ("zo", 1, 1), ("zc", 0, 1), ("chk4",),
    ("zc", 1, 1), ("zo", 0, 1), ("yend",), ("x3", 4), ("xo", 7), ("x3", 3), ("zo", 1, 2), ("zc", 0, 2), ("zc", 1, 2),
    ("zo", 0, 2), ("x3", 6), ("al1",), ("x3", 5), ("b2", 1), ("b2", 0), ("zc", 0, 3), ("x2", 0, 7), ("zo", 1, 3),
    ("x2", 1, 7), ("al2",), ("zc", 1, 3), ("zo", 0, 3), ("bend",), ("x3", 7), ("aend",),
)


def kernel(
    n_exp,
    tok_ref, ids_ref, gate_ref, dchk_ref, wg_hbm, wu_hbm, wd_hbm,
    out_ref, res_ref, alarm_ref,
    wg, wu, wd, x, p, acc_ga, acc_ua, acc_gb, acc_ub, hid, fin,
    sbuf, rbuf, bbuf, qbuf,
    xh, xf, zh, zf, yh, yf, bh, bf,
    racc, cs, cr, cf, zr, cc, es, er, gs, gr,
    w_sem, d_s, d_r, m_s, m_r,
    c_s, c_r, cc_s, cc_r, q_s, q_r, z_s, z_r, es_s, es_r, gs_s, gs_r,
):
    e = lax.axis_index("expert")
    t = lax.axis_index("tensor")
    d = lax.axis_index("dp")
    rows = x.shape[2]
    cols = x.shape[3]
    ff = wg.shape[1]
    toks = tok_ref.shape[0]
    na = rows * 3 // 5
    nb = rows - na
    A, A0, A1 = pl.ds(0, na), pl.ds(0, na // 2), pl.ds(na // 2, na // 2)
    B, B0, B1 = pl.ds(na, nb), pl.ds(na, nb // 2), pl.ds(na + nb // 2, nb // 2)

    def tz(o):
        return lax.rem(t + (o + 2 * NT), NT)

    def dx(o):
        return lax.rem(d + (o + 2 * NX), NX)

    def ex(o):
        return lax.rem(e + o, n_exp)

    y, core = lax.div(e, 2), lax.rem(e, 2)
    ny = n_exp // 2
    steps = [0, 1, ny - 1] + list(range(2, ny - 1))

    def source(j):
        return 2 * lax.rem(y + steps[j // 2], ny) + lax.rem(core + j % 2, 2)

    def expert_at(j):
        return 2 * lax.rem(y + ny - steps[j // 2], ny) + lax.rem(core + j % 2, 2)

    until_a = -(-na // CAP)
    from_b = na // CAP

    zdev = ((e, tz(1), d), (e, tz(-1), d))
    xdev = ((e, t, dx(1)), (e, t, dx(-1)))

    def copy(src, dst, ssem, rsem, dev):
        return pltpu.make_async_remote_copy(
            src_ref=src, dst_ref=dst, send_sem=ssem, recv_sem=rsem,
            device_id=dev, device_id_type=MESH,
        )

    def send(src, dst, ssem, rsem, dev):
        copy(src, dst, ssem, rsem, dev).start()

    def got(dst, ssem, rsem):
        copy(dst, dst, ssem, rsem, xdev[0]).wait_recv()

    def sent(src, ssem, rsem):
        copy(src, src, ssem, rsem, xdev[0]).wait_send()

    numbers = {}
    used = []

    def number(*key):
        return numbers.setdefault(key, len(numbers))

    def post(src, dst, side, dev, *key):
        n = number(side, *key)
        used.append((src, n))
        send(src, dst, m_s.at[n], m_r.at[n], dev)

    def take(dst, side, *key):
        n = number(side, *key)
        got(dst, m_s.at[n], m_r.at[n])

    def dot_t(a, b):
        return lax.dot_general(a, b, (((1,), (1,)), ((), ())), preferred_element_type=F32)

    def turned(row):
        return jnp.transpose(jnp.broadcast_to(row, (toks, toks)))[:, 0:1]

    w_copies = [
        pltpu.make_async_copy(src.at[:, pl.ds(i * cols, cols)], dst.at[i], w_sem.at[n, i])
        for n, (src, dst) in enumerate(((wg_hbm, wg), (wu_hbm, wu), (wd_hbm, wd)))
        for i in range(NT)
    ]
    for c in w_copies:
        c.start()
    barrier = pltpu.get_barrier_semaphore()
    for o in range(1, n_exp):
        pl.semaphore_signal(barrier, inc=1, device_id=(ex(o), t, d), device_id_type=MESH)
    for o in range(1, NT):
        pl.semaphore_signal(barrier, inc=1, device_id=(e, tz(o), d), device_id_type=MESH)
    for o in range(1, NX):
        pl.semaphore_signal(barrier, inc=1, device_id=(e, t, dx(o)), device_id_type=MESH)

    ids = ids_ref[...].astype(F32)
    ids_row = [jnp.broadcast_to(ids[k : k + 1], (8, toks)) for k in range(2)]
    iota_e = lax.broadcasted_iota(jnp.int32, (8, toks), 0).astype(F32)
    count = (ids_row[0] == iota_e).astype(F32) + (ids_row[1] == iota_e).astype(F32)
    above = lax.broadcasted_iota(jnp.int32, (toks, toks), 0) < lax.broadcasted_iota(jnp.int32, (toks, toks), 1)
    before = jnp.dot(count.astype(BF16), above.astype(F32).astype(BF16), preferred_element_type=F32)
    place = jnp.where(count > 0.5, before, -1.0)
    iota_p = lax.broadcasted_iota(jnp.int32, (CAP, toks), 0).astype(F32)
    pick = jnp.concatenate(
        [(iota_p == jnp.broadcast_to(place[i : i + 1], (CAP, toks))).astype(F32) for i in range(n_exp)], axis=0
    )
    slot_rows = jnp.dot(pick.astype(BF16), tok_ref[...], preferred_element_type=F32)
    sbuf[...] = slot_rows.reshape(n_exp, CAP, cols).astype(BF16)

    pl.semaphore_wait(barrier, n_exp - 1 + NT - 1 + NX - 1)

    for j in reversed(range(1, n_exp)):
        send(sbuf.at[expert_at(j)], rbuf.at[j], d_s.at[j - 1], d_r.at[j - 1], (expert_at(j), t, d))
    rbuf[0] = sbuf[e]
    acc_ga[...] = jnp.zeros_like(acc_ga)
    acc_ua[...] = jnp.zeros_like(acc_ua)
    acc_gb[...] = jnp.zeros_like(acc_gb)
    acc_ub[...] = jnp.zeros_like(acc_ub)
    for j in range(1, until_a):
        got(rbuf.at[j], d_s.at[j - 1], d_r.at[j - 1])
    x[t, d, A, :] = rbuf[0:until_a].astype(F32).reshape(until_a * CAP, cols)[0:na].astype(BF16)

    def mul_a(tp, dp):
        v = x[tp, dp, A, :]
        acc_ga[dp] += dot_t(v, wg[tp])
        acc_ua[dp] += dot_t(v, wu[tp])

    def mul_b(tp):
        v = x[tp, :, B, :].reshape(NX * nb, cols)
        acc_gb[...] += dot_t(v, wg[tp])
        acc_ub[...] += dot_t(v, wu[tp])

    def silu(g, u):
        return (g / (1.0 + jnp.exp(-g)) * u).astype(BF16)

    def act_a(dp):
        hid[dp, A, :] = silu(acc_ga[dp], acc_ua[dp])

    half_a, half_b = (A0, A1), (B0, B1)
    offs = (0, -1, 1, -2, 2, -3, 3, 4)
    sign = (-1, 1)

    def gather(kind, *key):
        if kind == "a1":
            i, h, s = key
            ref = x.at[tz(sign[i] * s), d, half_a[h]]
            take(ref, i, "a1", h, s)
            if s < 3 or (s == 3 and h == i):
                post(ref, ref, i, zdev[i], "a1", h, s + 1)
        elif kind == "s2":
            i, h, s = key
            ref = x.at[tz(sign[i] * s), d, half_a[h]]
            k = 7 if s == 4 else 2 * s - 1 + i
            for ii in range(2):
                post(ref, ref, ii, xdev[ii], "a2", k, h, 1)
        elif kind == "a2go":
            for i in range(2):
                for h in (i, 1 - i):
                    ref = x.at[t, d, half_a[h]]
                    post(ref, ref, i, xdev[i], "a2", 0, h, 1)
        elif kind == "b1go":
            for j in range(until_a, n_exp):
                got(rbuf.at[j], d_s.at[j - 1], d_r.at[j - 1])
            late = rbuf[from_b:n_exp].astype(F32).reshape((n_exp - from_b) * CAP, cols)
            x[t, d, B, :] = late[na - from_b * CAP :].astype(BF16)
            for i in range(2):
                for h in (i, 1 - i):
                    ref = x.at[t, d, half_b[h]]
                    post(ref, ref, i, xdev[i], "b1", h, 1)
        elif kind == "b1":
            i, h, s = key
            ref = x.at[t, dx(sign[i] * s), half_b[h]]
            take(ref, i, "b1", h, s)
            if s == 1 and h == i:
                post(ref, ref, i, xdev[i], "b1", h, 2)
        elif kind == "b2" and not key:
            for i in range(2):
                for h in (i, 1 - i):
                    ref = x.at[t, :, half_b[h]]
                    post(ref, ref, i, zdev[i], "b2", h, 1)
        elif kind == "b2":
            i, h, s = key
            ref = x.at[tz(sign[i] * s), :, half_b[h]]
            take(ref, i, "b2", h, s)
            if s < 3 or (s == 3 and h == i):
                post(ref, ref, i, zdev[i], "b2", h, s + 1)
        elif kind == "a2":
            i, k, h, s = key
            ref = x.at[tz(offs[k]), dx(sign[i] * s), half_a[h]]
            take(ref, i, "a2", k, h, s)
            if s == 1 and h == i:
                post(ref, ref, i, xdev[i], "a2", k, h, 2)
        elif kind == "ca":
            mul_a(tz(offs[key[0]]), dx(key[1]))
        elif kind == "cb":
            mul_b(tz(offs[key[0]]))
        elif kind == "act":
            act_a(dx(key[0]))
        else:
            hb = silu(acc_gb[...], acc_ub[...])
            for n in range(NX):
                hid[n, B, :] = hb[n * nb : (n + 1) * nb]

    for i in range(2):
        for h in (i, 1 - i):
            ref = x.at[t, d, half_a[h]]
            post(ref, ref, i, zdev[i], "a1", h, 1)
    for c in w_copies[: 2 * NT]:
        c.wait()
    for step in GATHER:
        gather(*step)

    for c in w_copies[2 * NT :]:
        c.wait()

    racc[...] = jnp.zeros_like(racc)

    def down(tp):
        def one(dp, carry):
            v = jnp.dot(hid[dp], wd[tp], preferred_element_type=F32).astype(BF16)
            p[tp, dp] = v
            v = v.astype(F32)
            racc[dp] += (v[:, 0:128] + v[:, 128:256]) + (v[:, 256:384] + v[:, 384:512]) if cols == 512 else v
            return carry

        lax.fori_loop(0, NX, one, 0)

    def add(tp, dp, span, *others):
        total = p[tp, dp, span, :].astype(F32)
        for o in others:
            total = total + o.astype(F32)
        p[tp, dp, span, :] = total.astype(BF16)

    far = (4, 3, -3, 2, -2, 1, -1, 0)
    side_a, side_b = ((A1, A0), (A0, A1)), ((B1, B0), (B0, B1))
    low_a, high_a = pl.ds(0, na // 2), pl.ds(na // 2, na // 2)
    low_b, high_b = pl.ds(0, nb // 2), pl.ds(nb // 2, nb // 2)
    slot_a, slot_b = ((high_a, low_a), (low_a, high_a)), ((high_b, low_b), (low_b, high_b))
    near = (1, -1)
    every = slice(None)

    def hand_back(first, last):
        if first == last:
            return
        done = fin[pl.ds(first * CAP, (last - first) * CAP), :]
        bbuf[first:last] = done.reshape(last - first, CAP, cols).astype(BF16)
        for j in reversed(range(max(first, 1), last)):
            send(bbuf.at[j], qbuf.at[e], q_s.at[j - 1], q_r.at[j - 1], (source(j), t, d))
        if first == 0:
            qbuf[e] = bbuf[0]

    def scatter(kind, *key):
        if kind == "down":
            (j,) = key
            tp = tz(far[j])
            down(tp)
            for i in range(2):
                post(p.at[tp, dx(2), side_a[i][0]], xh.at[j, i], i, xdev[i], "xh", j)
            if j == 0:
                for i in range(2):
                    post(p.at[tp, :, side_b[i][0]], yh.at[i], i, zdev[i], "yc", 0)
            if j in (1, 2):
                i = j - 1
                post(p.at[tp, :, side_b[i][1]], yf.at[0, i, :, slot_b[i][1]], i, zdev[i], "yo", 1)
        elif kind == "xo":
            (j,) = key
            for i in range(2):
                src = p.at[tz(far[j]), dx(near[i]), side_a[i][1]]
                post(src, xf.at[j, i, slot_a[i][1]], i, xdev[i], "xo", j)
        elif kind == "x2":
            i, j = key
            tp, dp = tz(far[j]), dx(near[i])
            take(xh.at[j, i], i, "xh", j)
            add(tp, dp, side_a[i][0], xh[j, i])
            post(p.at[tp, dp, side_a[i][0]], xf.at[j, i, slot_a[i][0]], i, xdev[i], "xf", j)
        elif kind == "x3":
            (j,) = key
            for i in range(2):
                take(xf.at[j, i, slot_a[i][1]], i, "xo", j)
                take(xf.at[j, i, slot_a[i][0]], i, "xf", j)
            add(tz(far[j]), d, A, xf[j, 0], xf[j, 1])
        elif kind in ("yc", "yo"):
            i, s = key
            n = 0 if kind == "yc" else 1
            tp = tz(near[i] * (4 - s))
            src = yh.at[i] if s == 1 else yf.at[s - 2, i, :, slot_b[i][n]]
            take(src, i, kind, s - 1)
            add(tp, every, side_b[i][n], src[...])
            post(p.at[tp, :, side_b[i][n]], yf.at[s - 1, i, :, slot_b[i][n]], i, zdev[i], kind, s)
        elif kind == "yend":
            for i in range(2):
                take(yf.at[2, i, :, slot_b[i][0]], i, "yc", 3)
                take(yf.at[2, i, :, slot_b[i][1]], i, "yo", 3)
            add(t, every, B, yf[2, 0], yf[2, 1])
            for i in range(2):
                post(p.at[t, dx(2), side_b[i][0]], bh.at[i], i, xdev[i], "bh")
            for i in range(2):
                post(p.at[t, dx(near[i]), side_b[i][1]], bf.at[i, slot_b[i][1]], i, xdev[i], "bo")
        elif kind == "b2":
            (i,) = key
            take(bh.at[i], i, "bh")
            add(t, dx(near[i]), side_b[i][0], bh[i])
            post(p.at[t, dx(near[i]), side_b[i][0]], bf.at[i, slot_b[i][0]], i, xdev[i], "bf")
        elif kind == "zgo":
            for i in range(2):
                post(p.at[tz(4), d, side_a[i][0]], zh.at[i], i, zdev[i], "zc", 0)
        elif kind in ("zc", "zo"):
            i, s = key
            n = 0 if kind == "zc" else 1
            tp = tz(near[i] * (4 - s))
            if kind == "zc" or s > 1:
                src = zh.at[i] if s == 1 else zf.at[s - 2, i, slot_a[i][n]]
                take(src, i, kind, s - 1)
                add(tp, d, side_a[i][n], src[...])
            post(p.at[tp, d, side_a[i][n]], zf.at[s - 1, i, slot_a[i][n]], i, zdev[i], kind, s)
        elif kind == "aend":
            for i in range(2):
                take(zf.at[2, i, slot_a[i][0]], i, "zc", 3)
                take(zf.at[2, i, slot_a[i][1]], i, "zo", 3)
            fin[A, :] = p[t, d, A, :].astype(F32) + zf[2, 0].astype(F32) + zf[2, 1].astype(F32)
            hand_back(0, until_a)
        elif kind == "bend":
            for i in range(2):
                take(bf.at[i, slot_b[i][1]], i, "bo")
                take(bf.at[i, slot_b[i][0]], i, "bf")
            fin[B, :] = p[t, d, B, :].astype(F32) + bf[0].astype(F32) + bf[1].astype(F32)
            hand_back(until_a, n_exp)
        else:
            CHECKS[kind]()

    def chk():
        dc = jnp.broadcast_to(dchk_ref[...].astype(F32), (16, ff)).astype(BF16)
        ones = jnp.ones((8, racc.shape[2]), F32)
        for i in range(NX):
            sums = lax.dot_general(
                ones, racc[i], (((1,), (1,)), ((), ())), preferred_element_type=F32, precision=lax.Precision.HIGHEST
            )
            cs[i] = (sums - dot_t(dc, hid[i])[0:8])[0:1]
        for o in range(1, NX):
            send(cs.at[dx(o)], cr.at[o - 1], c_s.at[o - 1], c_r.at[o - 1], (e, t, dx(o)))

    def chk2():
        for o in range(1, NX):
            got(cr.at[o - 1], c_s.at[o - 1], c_r.at[o - 1])
        cf[0] = cs[d] + cr[0] + cr[1] + cr[2]
        zr[t] = cf[0]
        for o in range(1, NT):
            send(cf.at[0], zr.at[t], z_s.at[o - 1], z_r.at[o - 1], (e, tz(o), d))

    def chk3():
        for o in range(1, NT):
            got(zr.at[tz(-o)], z_s.at[o - 1], z_r.at[o - 1])
        total = zr[0]
        for i in range(1, NT):
            total = total + zr[i]
        cf[1] = total
        cc[0] = total
        for j in range(1, n_exp):
            send(cf.at[1], cc.at[j], cc_s.at[j - 1], cc_r.at[j - 1], (source(j), t, d))

    iota_s = lax.broadcasted_iota(jnp.int32, (toks, rows), 1).astype(F32)
    route = {}

    def chk4():
        iota_l = lax.broadcasted_iota(jnp.int32, (toks, toks), 1).astype(F32)
        col = [turned(ids[k : k + 1]) for k in range(2)]
        left = [(col[k] == iota_l).astype(F32) for k in range(2)]
        below = lax.broadcasted_iota(jnp.int32, (toks, toks), 1) < lax.broadcasted_iota(jnp.int32, (toks, toks), 0)
        before_col = jnp.dot(
            below.astype(F32).astype(BF16), (left[0] + left[1]).astype(BF16), preferred_element_type=F32
        )
        pos = [jnp.sum(left[k] * before_col, axis=1, keepdims=True) for k in range(2)]
        gates = gate_ref[...].astype(F32)
        gate_sum = gates[0:1] + gates[1:2]
        weight = [turned(gates[k : k + 1] / gate_sum) for k in range(2)]
        for j in range(1, n_exp):
            got(cc.at[j], cc_s.at[j - 1], cc_r.at[j - 1])
        diff = jnp.zeros((toks, 1), F32)
        for k in range(2):
            row = jnp.zeros((toks, rows), F32)
            place = pos[k]
            for j in range(n_exp):
                here = col[k] == expert_at(j).astype(F32)
                row = row + jnp.where(here, jnp.broadcast_to(cc[j], (toks, rows)), 0.0)
                place = place + jnp.where(here, float(CAP * j), 0.0)
            picked = jnp.where(iota_s == place, row, 0.0)
            diff = diff + weight[k] * jnp.sum(picked, axis=1, keepdims=True)
        residual = jnp.transpose(jnp.broadcast_to(diff, (toks, toks)))[0:1] * (1.0 / math.sqrt(D))
        res_ref[...] = residual
        score = jnp.broadcast_to(jnp.sum(residual * residual, axis=1, keepdims=True), (1, toks))
        es[...] = score
        for o in range(1, NX):
            send(es, er.at[d], es_s.at[o - 1], es_r.at[o - 1], (e, t, dx(o)))
        er[d] = score
        route["weight"] = weight
        route["slot"] = [col[k] * float(CAP) + pos[k] for k in range(2)]

    def al1():
        for o in range(1, NX):
            got(er.at[dx(-o)], es_s.at[o - 1], es_r.at[o - 1])
        score = er[0]
        for i in range(1, NX):
            score = score + er[i]
        gs[...] = score
        for o in range(1, n_exp):
            send(gs, gr.at[e], gs_s.at[o - 1], gs_r.at[o - 1], (ex(o), t, d))
        gr[e] = score

    def al2():
        for o in range(1, n_exp):
            got(gr.at[ex(n_exp - o)], gs_s.at[o - 1], gs_r.at[o - 1])
        score = gr[0]
        for i in range(1, n_exp):
            score = score + gr[i]
        alarm_ref[...] = score[0:1, 0:1] * (1.0 / (toks * n_exp * NX))

    CHECKS = {"chk": chk, "chk2": chk2, "chk3": chk3, "chk4": chk4, "al1": al1, "al2": al2}
    for step in SCATTER:
        scatter(*step)

    for j in range(1, n_exp):
        got(qbuf.at[expert_at(j)], q_s.at[j - 1], q_r.at[j - 1])
    back = qbuf[...].astype(F32).reshape(rows, cols).astype(BF16)
    combined = jnp.zeros((toks, cols), F32)
    for k in range(2):
        sel = (iota_s == route["slot"][k]).astype(F32).astype(BF16)
        combined = combined + route["weight"][k] * jnp.dot(sel, back, preferred_element_type=F32)
    out_ref[...] = combined

    for o in range(n_exp - 1):
        sent(sbuf.at[0], d_s.at[o], d_r.at[o])
        sent(cf.at[1], cc_s.at[o], cc_r.at[o])
        sent(bbuf.at[0], q_s.at[o], q_r.at[o])
        sent(gs, gs_s.at[o], gs_r.at[o])
    for o in range(NX - 1):
        sent(cs.at[0], c_s.at[o], c_r.at[o])
        sent(es, es_s.at[o], es_r.at[o])
    for o in range(NT - 1):
        sent(cf.at[0], z_s.at[o], z_r.at[o])
    for ref, n in used:
        sent(ref, m_s.at[n], m_r.at[n])


def body(tokens, expert_ids, gate_fixed, w_gate, w_up, w_down, down_check):
    n_exp = lax.axis_size("expert")
    toks, cols = tokens.shape
    ff = w_gate.shape[2]
    rows = n_exp * CAP
    na = rows * 3 // 5
    nb = rows - na
    dma = lambda *s: pltpu.SemaphoreType.DMA(s)
    both = lambda *s: [dma(*s), dma(*s)]
    vm = pltpu.VMEM
    scratch = [
        vm((NT, ff, cols), BF16), vm((NT, ff, cols), BF16), vm((NT, ff, cols), BF16),
        vm((NT, NX, rows, cols), BF16), vm((NT, NX, rows, cols), BF16),
        vm((NX, na, ff), F32), vm((NX, na, ff), F32), vm((NX * nb, ff), F32), vm((NX * nb, ff), F32),
        vm((NX, rows, ff), BF16), vm((rows, cols), F32),
        vm((n_exp, CAP, cols), BF16), vm((n_exp, CAP, cols), BF16),
        vm((n_exp, CAP, cols), BF16), vm((n_exp, CAP, cols), BF16),
        vm((NT, 2, na // 2, cols), BF16), vm((NT, 2, na, cols), BF16),
        vm((2, na // 2, cols), BF16), vm((3, 2, na, cols), BF16),
        vm((2, NX, nb // 2, cols), BF16), vm((3, 2, NX, nb, cols), BF16),
        vm((2, nb // 2, cols), BF16), vm((2, nb, cols), BF16),
        vm((NX, rows, min(cols, 128)), F32),
        vm((NX, 1, rows), F32), vm((NX - 1, 1, rows), F32), vm((2, 1, rows), F32), vm((NT, 1, rows), F32),
        vm((n_exp, 1, rows), F32), vm((1, toks), F32), vm((NX, 1, toks), F32),
        vm((1, toks), F32), vm((n_exp, 1, toks), F32),
        dma(3, NT), *both(n_exp - 1), *both(MESSAGES),
        *both(NX - 1), *both(n_exp - 1), *both(n_exp - 1), *both(NT - 1), *both(NX - 1), *both(n_exp - 1),
    ]
    vmem = pl.BlockSpec(memory_space=pltpu.VMEM)
    hbm = pl.BlockSpec(memory_space=pl.ANY)
    mix, residual, alarm = pl.pallas_call(
        functools.partial(kernel, n_exp),
        out_shape=(
            jax.ShapeDtypeStruct((toks, cols), F32),
            jax.ShapeDtypeStruct((1, toks), F32),
            jax.ShapeDtypeStruct((1, 1), F32),
        ),
        in_specs=[vmem, vmem, vmem, vmem, hbm, hbm, hbm],
        out_specs=(vmem, vmem, vmem),
        scratch_shapes=scratch,
        compiler_params=pltpu.CompilerParams(
            collective_id=0, has_side_effects=True, vmem_limit_bytes=66_000_000
        ),
    )(
        tokens, expert_ids.T, gate_fixed.T, down_check,
        w_gate[0].T, w_up[0].T, w_down[0],
    )
    return mix, residual.reshape(toks), alarm.reshape(())


def solution(mesh):
    return jax.shard_map(
        body,
        mesh=mesh,
        in_specs=(
            P(("expert", "dp"), "tensor"),
            P(("expert", "dp"), None),
            P(("expert", "dp"), None),
            P("expert", None, ("tensor", "dp")),
            P("expert", None, ("tensor", "dp")),
            P("expert", ("tensor", "dp"), None),
            P("expert", ("tensor", "dp")),
        ),
        out_specs=(P(("expert", "dp"), "tensor"), P(("expert", "dp")), P()),
        check_vma=False,
    )
```

```python
import functools
import math

import jax
import jax.numpy as jnp
from jax import lax
from jax.experimental import pallas as pl
from jax.experimental.pallas import tpu as pltpu
from jax.sharding import PartitionSpec as P

D = 4096
CAP = 40
MESH = pl.DeviceIdType.MESH
NT = 8
NX = 4
MESSAGES = 164
F32 = jnp.float32
BF16 = jnp.bfloat16

GATHER = (
    ("a2go",), ("b1go",), ("a1", 1, 1, 1), ("a1", 0, 0, 1), ("s2", 0, 0, 1), ("a1", 1, 0, 1), ("a1", 0, 1, 1),
    ("a2", 1, 0, 0, 1), ("b1", 1, 1, 1), ("b1", 0, 0, 1), ("a1", 1, 1, 2), ("a1", 0, 0, 2), ("b1", 1, 0, 1),
    ("s2", 1, 1, 2), ("a1", 1, 0, 2), ("a1", 0, 1, 2), ("a2", 1, 0, 1, 1), ("s2", 1, 0, 2), ("ca", 4, 0),
    ("s2", 0, 1, 1), ("b1", 0, 1, 1), ("b1", 0, 0, 2), ("b1", 1, 1, 2), ("b2",), ("a1", 0, 1, 3), ("s2", 0, 0, 2),
    ("ca", 1, 0), ("ca", 0, 0), ("s2", 1, 1, 1), ("a2", 1, 1, 1, 1), ("s2", 1, 0, 1), ("cb", 0), ("a1", 0, 0, 3),
    ("s2", 0, 0, 3), ("s2", 0, 1, 2), ("a2", 1, 3, 0, 1), ("b2", 0, 0, 1), ("a2", 0, 4, 1, 1), ("a2", 0, 1, 1, 1),
    ("a1", 1, 1, 3), ("a2", 0, 2, 0, 1), ("s2", 0, 1, 3), ("b2", 1, 1, 1), ("ca", 2, 0), ("a1", 1, 0, 3),
    ("b2", 1, 0, 1), ("a2", 1, 1, 0, 1), ("a2", 0, 2, 1, 1), ("a2", 0, 5, 0, 1), ("cb", 2), ("b2", 0, 1, 1),
    ("a1", 1, 1, 4), ("s2", 1, 0, 3), ("ca", 2, -1), ("a2", 0, 0, 1, 1), ("a2", 0, 4, 0, 1), ("ca", 4, -1),
    ("ca", 5, 0), ("a2", 0, 1, 0, 1), ("ca", 3, 0), ("a1", 0, 0, 4), ("cb", 1), ("a2", 1, 4, 1, 1),
    ("a2", 0, 3, 1, 1), ("ca", 6, 0), ("a2", 0, 0, 0, 1), ("a2", 1, 2, 0, 1), ("a2", 0, 5, 1, 1), ("a2", 1, 1, 1, 2),
    ("b2", 0, 0, 2), ("a2", 1, 5, 0, 1), ("a2", 1, 4, 0, 1), ("s2", 1, 1, 3), ("ca", 0, 1), ("a2", 1, 2, 1, 1),
    ("ca", 0, -1), ("a2", 1, 5, 1, 1), ("a2", 1, 3, 1, 1), ("ca", 4, 1), ("a2", 1, 0, 1, 2), ("ca", 7, 0),
    ("s2", 1, 1, 4), ("s2", 0, 0, 4), ("b2", 1, 1, 2), ("ca", 1, 1), ("act", 0), ("a2", 1, 4, 1, 2),
    ("a2", 0, 5, 0, 2), ("b2", 0, 1, 2), ("a2", 0, 4, 0, 2), ("a2", 1, 6, 0, 1), ("b2", 1, 0, 2), ("cb", 4),
    ("ca", 4, 2), ("ca", 5, -1), ("a2", 0, 6, 0, 1), ("ca", 3, 1), ("cb", 3), ("a2", 0, 1, 0, 2), ("ca", 5, 1),
    ("a2", 0, 0, 0, 2), ("a2", 0, 3, 0, 1), ("ca", 1, -1), ("a2", 1, 2, 1, 2), ("ca", 3, -1), ("a2", 0, 2, 0, 2),
    ("ca", 1, 2), ("ca", 2, 1), ("b2", 0, 0, 3), ("a2", 1, 5, 1, 2), ("b2", 1, 1, 3), ("a2", 0, 6, 1, 1),
    ("ca", 6, -1), ("ca", 0, 2), ("a2", 1, 6, 1, 1), ("ca", 5, 2), ("ca", 2, 2), ("ca", 6, 1), ("b2", 0, 1, 3),
    ("cb", 5), ("a2", 1, 7, 1, 1), ("a2", 0, 7, 0, 1), ("b2", 1, 0, 3), ("cb", 6), ("a2", 0, 7, 1, 1), ("ca", 7, -1),
    ("a2", 1, 7, 0, 1), ("a2", 1, 3, 1, 2), ("ca", 7, 1), ("act", 1), ("a2", 0, 6, 0, 2), ("act", -1),
    ("a2", 1, 6, 1, 2), ("ca", 6, 2), ("a2", 0, 3, 0, 2), ("ca", 3, 2), ("b2", 1, 1, 4), ("b2", 0, 0, 4), ("cb", 7),
    ("a2", 0, 7, 0, 2), ("a2", 1, 7, 1, 2), ("ca", 7, 2), ("actb",), ("act", 2),
)

SCATTER = (
    ("down", 0), ("down", 1), ("down", 2), ("x2", 0, 0), ("down", 3), ("xo", 0), ("down", 4), ("down", 5),
    ("down", 6), ("yc", 1, 1), ("x2", 1, 2), ("x2", 1, 0), ("yc", 0, 1), ("down", 7), ("chk",), ("xo", 2),
    ("yo", 1, 2), ("xo", 4), ("x2", 0, 2), ("yo", 0, 2), ("x2", 0, 1), ("yc", 0, 2), ("yc", 1, 2), ("x3", 0),
    ("x2", 1, 3), ("x2", 1, 4), ("x2", 0, 4), ("xo", 3), ("yo", 0, 3), ("x2", 1, 1), ("chk2",), ("zgo",),
    ("yo", 1, 3), ("x2", 0, 6), ("yc", 1, 3), ("xo", 1), ("x3", 4), ("x3", 2), ("x2", 0, 3), ("x2", 1, 6),
    ("zo", 1, 1), ("yc", 0, 3), ("xo", 6), ("xo", 5), ("chk3",), ("x3", 1), ("zo", 0, 1), ("chk4",), ("zc", 0, 1),
    ("zc", 1, 1), ("x2", 1, 5), ("x2", 0, 5), ("yend",), ("x3", 3), ("x2", 0, 7), ("x2", 1, 7), ("x3", 6),
    ("zo", 0, 2), ("zo", 1, 2), ("zc", 0, 2), ("zc", 1, 2), ("al1",), ("b2", 1), ("b2", 0), ("x3", 5), ("zo", 0, 3),
    ("zo", 1, 3), ("xo", 7), ("al2",), ("zc", 0, 3), ("zc", 1, 3), ("bend",), ("x3", 7), ("aend",),
)


def kernel(
    n_exp,
    tok_ref, ids_ref, gate_ref, dchk_ref, wg_hbm, wu_hbm, wd_hbm,
    qbuf, aux_ref,
    wg, wu, wd, x, p, acc_ga, acc_ua, acc_gb, acc_ub, hid, fin,
    sbuf, rbuf, bbuf,
    xh, xf, zh, zf, yh, yf, bh, bf,
    racc, cs, cr, cf, zr, cc, es, er, gs, gr,
    w_sem, d_s, d_r, m_s, m_r,
    c_s, c_r, cc_s, cc_r, q_s, q_r, z_s, z_r, es_s, es_r, gs_s, gs_r,
):
    e = lax.axis_index("expert")
    t = lax.axis_index("tensor")
    d = lax.axis_index("dp")
    rows = x.shape[2]
    cols = x.shape[3]
    ff = wg.shape[1]
    toks = tok_ref.shape[0]
    na = rows * 3 // 5
    nb = rows - na
    A, A0, A1 = pl.ds(0, na), pl.ds(0, na // 2), pl.ds(na // 2, na // 2)
    B, B0, B1 = pl.ds(na, nb), pl.ds(na, nb // 2), pl.ds(na + nb // 2, nb // 2)

    def tz(o):
        return lax.rem(t + (o + 2 * NT), NT)

    def dx(o):
        return lax.rem(d + (o + 2 * NX), NX)

    def ex(o):
        return lax.rem(e + o, n_exp)

    y, core = lax.div(e, 2), lax.rem(e, 2)
    ny = n_exp // 2
    steps = [0, 1, ny - 1] + list(range(2, ny - 1))

    def source(j):
        return 2 * lax.rem(y + steps[j // 2], ny) + lax.rem(core + j % 2, 2)

    def expert_at(j):
        return 2 * lax.rem(y + ny - steps[j // 2], ny) + lax.rem(core + j % 2, 2)

    until_a = -(-na // CAP)
    from_b = na // CAP

    zdev = ((e, tz(1), d), (e, tz(-1), d))
    xdev = ((e, t, dx(1)), (e, t, dx(-1)))

    def copy(src, dst, ssem, rsem, dev):
        return pltpu.make_async_remote_copy(
            src_ref=src, dst_ref=dst, send_sem=ssem, recv_sem=rsem,
            device_id=dev, device_id_type=MESH,
        )

    def send(src, dst, ssem, rsem, dev):
        copy(src, dst, ssem, rsem, dev).start()

    def got(dst, ssem, rsem):
        copy(dst, dst, ssem, rsem, xdev[0]).wait_recv()

    def sent(src, ssem, rsem):
        copy(src, src, ssem, rsem, xdev[0]).wait_send()

    numbers = {}
    used = []

    def number(*key):
        return numbers.setdefault(key, len(numbers))

    def post(src, dst, side, dev, *key):
        n = number(side, *key)
        used.append((src, n))
        send(src, dst, m_s.at[n], m_r.at[n], dev)

    def take(dst, side, *key):
        n = number(side, *key)
        got(dst, m_s.at[n], m_r.at[n])

    def dot_t(a, b):
        return lax.dot_general(a, b, (((1,), (1,)), ((), ())), preferred_element_type=F32)

    def turned(row):
        return jnp.transpose(jnp.broadcast_to(row, (toks, toks)))[:, 0:1]

    w_copies = [
        pltpu.make_async_copy(src.at[:, pl.ds(i * cols, cols)], dst.at[i], w_sem.at[n, i])
        for n, (src, dst) in enumerate(((wg_hbm, wg), (wu_hbm, wu), (wd_hbm, wd)))
        for i in range(NT)
    ]
    for c in w_copies:
        c.start()
    barrier = pltpu.get_barrier_semaphore()
    for o in range(1, n_exp):
        pl.semaphore_signal(barrier, inc=1, device_id=(ex(o), t, d), device_id_type=MESH)
    for o in range(1, NT):
        pl.semaphore_signal(barrier, inc=1, device_id=(e, tz(o), d), device_id_type=MESH)
    for o in range(1, NX):
        pl.semaphore_signal(barrier, inc=1, device_id=(e, t, dx(o)), device_id_type=MESH)

    ids = ids_ref[...].astype(F32)
    ids_row = [jnp.broadcast_to(ids[k : k + 1], (8, toks)) for k in range(2)]
    iota_e = lax.broadcasted_iota(jnp.int32, (8, toks), 0).astype(F32)
    count = (ids_row[0] == iota_e).astype(F32) + (ids_row[1] == iota_e).astype(F32)
    above = lax.broadcasted_iota(jnp.int32, (toks, toks), 0) < lax.broadcasted_iota(jnp.int32, (toks, toks), 1)
    before = jnp.dot(count.astype(BF16), above.astype(F32).astype(BF16), preferred_element_type=F32)
    place = jnp.where(count > 0.5, before, -1.0)
    iota_p = lax.broadcasted_iota(jnp.int32, (CAP, toks), 0).astype(F32)
    pick = jnp.concatenate(
        [(iota_p == jnp.broadcast_to(place[i : i + 1], (CAP, toks))).astype(F32) for i in range(n_exp)], axis=0
    )
    slot_rows = jnp.dot(pick.astype(BF16), tok_ref[...], preferred_element_type=F32)
    sbuf[...] = slot_rows.reshape(n_exp, CAP, cols).astype(BF16)

    pl.semaphore_wait(barrier, n_exp - 1 + NT - 1 + NX - 1)

    for j in reversed(range(1, n_exp)):
        send(sbuf.at[expert_at(j)], rbuf.at[j], d_s.at[j - 1], d_r.at[j - 1], (expert_at(j), t, d))
    rbuf[0] = sbuf[e]
    acc_ga[...] = jnp.zeros_like(acc_ga)
    acc_ua[...] = jnp.zeros_like(acc_ua)
    acc_gb[...] = jnp.zeros_like(acc_gb)
    acc_ub[...] = jnp.zeros_like(acc_ub)
    for j in range(1, until_a):
        got(rbuf.at[j], d_s.at[j - 1], d_r.at[j - 1])
    x[t, d, A, :] = rbuf[0:until_a].astype(F32).reshape(until_a * CAP, cols)[0:na].astype(BF16)

    def mul_a(tp, dp):
        v = x[tp, dp, A, :]
        acc_ga[dp] += dot_t(v, wg[tp])
        acc_ua[dp] += dot_t(v, wu[tp])

    def mul_b(tp):
        v = x[tp, :, B, :].reshape(NX * nb, cols)
        acc_gb[...] += dot_t(v, wg[tp])
        acc_ub[...] += dot_t(v, wu[tp])

    def silu(g, u):
        return (g / (1.0 + jnp.exp(-g)) * u).astype(BF16)

    def act_a(dp):
        hid[dp, A, :] = silu(acc_ga[dp], acc_ua[dp])

    half_a, half_b = (A0, A1), (B0, B1)
    offs = (0, -1, 1, -2, 2, -3, 3, 4)
    sign = (-1, 1)

    def gather(kind, *key):
        if kind == "a1":
            i, h, s = key
            ref = x.at[tz(sign[i] * s), d, half_a[h]]
            take(ref, i, "a1", h, s)
            if s < 3 or (s == 3 and h == i):
                post(ref, ref, i, zdev[i], "a1", h, s + 1)
        elif kind == "s2":
            i, h, s = key
            ref = x.at[tz(sign[i] * s), d, half_a[h]]
            k = 7 if s == 4 else 2 * s - 1 + i
            for ii in range(2):
                post(ref, ref, ii, xdev[ii], "a2", k, h, 1)
        elif kind == "a2go":
            for i in range(2):
                for h in (i, 1 - i):
                    ref = x.at[t, d, half_a[h]]
                    post(ref, ref, i, xdev[i], "a2", 0, h, 1)
        elif kind == "b1go":
            for j in range(until_a, n_exp):
                got(rbuf.at[j], d_s.at[j - 1], d_r.at[j - 1])
            late = rbuf[from_b:n_exp].astype(F32).reshape((n_exp - from_b) * CAP, cols)
            x[t, d, B, :] = late[na - from_b * CAP :].astype(BF16)
            for i in range(2):
                for h in (i, 1 - i):
                    ref = x.at[t, d, half_b[h]]
                    post(ref, ref, i, xdev[i], "b1", h, 1)
        elif kind == "b1":
            i, h, s = key
            ref = x.at[t, dx(sign[i] * s), half_b[h]]
            take(ref, i, "b1", h, s)
            if s == 1 and h == i:
                post(ref, ref, i, xdev[i], "b1", h, 2)
        elif kind == "b2" and not key:
            for i in range(2):
                for h in (i, 1 - i):
                    ref = x.at[t, :, half_b[h]]
                    post(ref, ref, i, zdev[i], "b2", h, 1)
        elif kind == "b2":
            i, h, s = key
            ref = x.at[tz(sign[i] * s), :, half_b[h]]
            take(ref, i, "b2", h, s)
            if s < 3 or (s == 3 and h == i):
                post(ref, ref, i, zdev[i], "b2", h, s + 1)
        elif kind == "a2":
            i, k, h, s = key
            ref = x.at[tz(offs[k]), dx(sign[i] * s), half_a[h]]
            take(ref, i, "a2", k, h, s)
            if s == 1 and h == i:
                post(ref, ref, i, xdev[i], "a2", k, h, 2)
        elif kind == "ca":
            mul_a(tz(offs[key[0]]), dx(key[1]))
        elif kind == "cb":
            mul_b(tz(offs[key[0]]))
        elif kind == "act":
            act_a(dx(key[0]))
        else:
            hb = silu(acc_gb[...], acc_ub[...])
            for n in range(NX):
                hid[n, B, :] = hb[n * nb : (n + 1) * nb]

    for i in range(2):
        for h in (i, 1 - i):
            ref = x.at[t, d, half_a[h]]
            post(ref, ref, i, zdev[i], "a1", h, 1)
    for c in w_copies[: 2 * NT]:
        c.wait()
    for step in GATHER:
        gather(*step)

    for c in w_copies[2 * NT :]:
        c.wait()

    def down(tp):
        def one(dp, carry):
            v = jnp.dot(hid[dp], wd[tp], preferred_element_type=F32).astype(BF16)
            p[tp, dp] = v
            v = v.astype(F32)
            racc[dp] += (v[:, 0:128] + v[:, 128:256]) + (v[:, 256:384] + v[:, 384:512]) if cols == 512 else v
            return carry

        lax.fori_loop(0, NX, one, 0)

    def down_rows(tp, dp, span):
        v = jnp.dot(hid[dp, span, :], wd[tp], preferred_element_type=F32).astype(BF16)
        p[tp, dp, span, :] = v
        v = v.astype(F32)
        racc[dp, span, :] = (v[:, 0:128] + v[:, 128:256]) + (v[:, 256:384] + v[:, 384:512]) if cols == 512 else v

    def add(tp, dp, span, *others):
        total = p[tp, dp, span, :].astype(F32)
        for o in others:
            total = total + o.astype(F32)
        p[tp, dp, span, :] = total.astype(BF16)

    far = (4, 3, -3, 2, -2, 1, -1, 0)
    side_a, side_b = ((A1, A0), (A0, A1)), ((B1, B0), (B0, B1))
    low_a, high_a = pl.ds(0, na // 2), pl.ds(na // 2, na // 2)
    low_b, high_b = pl.ds(0, nb // 2), pl.ds(nb // 2, nb // 2)
    slot_a, slot_b = ((high_a, low_a), (low_a, high_a)), ((high_b, low_b), (low_b, high_b))
    near = (1, -1)
    every = slice(None)

    def hand_back(first, last):
        if first == last:
            return
        done = fin[pl.ds(first * CAP, (last - first) * CAP), :]
        bbuf[first:last] = done.reshape(last - first, CAP, cols).astype(BF16)
        for j in reversed(range(max(first, 1), last)):
            send(bbuf.at[j], qbuf.at[e], q_s.at[j - 1], q_r.at[j - 1], (source(j), t, d))
        if first == 0:
            qbuf[e] = bbuf[0]

    def scatter(kind, *key):
        if kind == "down":
            (j,) = key
            tp = tz(far[j])
            if j == 0:
                for n in range(NX):
                    down_rows(tp, n, B)
                for i in range(2):
                    post(p.at[tp, :, side_b[i][0]], yh.at[i], i, zdev[i], "yc", 0)
                down_rows(tp, dx(2), A)
            else:
                down(tp)
            for i in range(2):
                post(p.at[tp, dx(2), side_a[i][0]], xh.at[j, i], i, xdev[i], "xh", j)
            if j == 0:
                for n in (1, -1, 0):
                    down_rows(tp, dx(n), A)
            if j in (1, 2):
                i = j - 1
                post(p.at[tp, :, side_b[i][1]], yf.at[0, i, :, slot_b[i][1]], i, zdev[i], "yo", 1)
        elif kind == "xo":
            (j,) = key
            for i in range(2):
                src = p.at[tz(far[j]), dx(near[i]), side_a[i][1]]
                post(src, xf.at[j, i, slot_a[i][1]], i, xdev[i], "xo", j)
        elif kind == "x2":
            i, j = key
            tp, dp = tz(far[j]), dx(near[i])
            take(xh.at[j, i], i, "xh", j)
            add(tp, dp, side_a[i][0], xh[j, i])
            post(p.at[tp, dp, side_a[i][0]], xf.at[j, i, slot_a[i][0]], i, xdev[i], "xf", j)
        elif kind == "x3":
            (j,) = key
            for i in range(2):
                take(xf.at[j, i, slot_a[i][1]], i, "xo", j)
                take(xf.at[j, i, slot_a[i][0]], i, "xf", j)
            add(tz(far[j]), d, A, xf[j, 0], xf[j, 1])
        elif kind in ("yc", "yo"):
            i, s = key
            n = 0 if kind == "yc" else 1
            tp = tz(near[i] * (4 - s))
            src = yh.at[i] if s == 1 else yf.at[s - 2, i, :, slot_b[i][n]]
            take(src, i, kind, s - 1)
            add(tp, every, side_b[i][n], src[...])
            post(p.at[tp, :, side_b[i][n]], yf.at[s - 1, i, :, slot_b[i][n]], i, zdev[i], kind, s)
        elif kind == "yend":
            for i in range(2):
                take(yf.at[2, i, :, slot_b[i][0]], i, "yc", 3)
                take(yf.at[2, i, :, slot_b[i][1]], i, "yo", 3)
            add(t, every, B, yf[2, 0], yf[2, 1])
            for i in range(2):
                post(p.at[t, dx(2), side_b[i][0]], bh.at[i], i, xdev[i], "bh")
            for i in range(2):
                post(p.at[t, dx(near[i]), side_b[i][1]], bf.at[i, slot_b[i][1]], i, xdev[i], "bo")
        elif kind == "b2":
            (i,) = key
            take(bh.at[i], i, "bh")
            add(t, dx(near[i]), side_b[i][0], bh[i])
            post(p.at[t, dx(near[i]), side_b[i][0]], bf.at[i, slot_b[i][0]], i, xdev[i], "bf")
        elif kind == "zgo":
            for i in range(2):
                post(p.at[tz(4), d, side_a[i][0]], zh.at[i], i, zdev[i], "zc", 0)
        elif kind in ("zc", "zo"):
            i, s = key
            n = 0 if kind == "zc" else 1
            tp = tz(near[i] * (4 - s))
            if kind == "zc" or s > 1:
                src = zh.at[i] if s == 1 else zf.at[s - 2, i, slot_a[i][n]]
                take(src, i, kind, s - 1)
                add(tp, d, side_a[i][n], src[...])
            post(p.at[tp, d, side_a[i][n]], zf.at[s - 1, i, slot_a[i][n]], i, zdev[i], kind, s)
        elif kind == "aend":
            for i in range(2):
                take(zf.at[2, i, slot_a[i][0]], i, "zc", 3)
                take(zf.at[2, i, slot_a[i][1]], i, "zo", 3)
            fin[A, :] = p[t, d, A, :].astype(F32) + zf[2, 0].astype(F32) + zf[2, 1].astype(F32)
            hand_back(0, until_a)
        elif kind == "bend":
            for i in range(2):
                take(bf.at[i, slot_b[i][1]], i, "bo")
                take(bf.at[i, slot_b[i][0]], i, "bf")
            fin[B, :] = p[t, d, B, :].astype(F32) + bf[0].astype(F32) + bf[1].astype(F32)
            hand_back(until_a, n_exp)
        else:
            CHECKS[kind]()

    def chk():
        dc = jnp.broadcast_to(dchk_ref[...].astype(F32), (16, ff)).astype(BF16)
        ones = jnp.ones((8, racc.shape[2]), F32)
        for i in range(NX):
            sums = lax.dot_general(
                ones, racc[i], (((1,), (1,)), ((), ())), preferred_element_type=F32, precision=lax.Precision.HIGHEST
            )
            cs[i] = (sums - dot_t(dc, hid[i])[0:8])[0:1]
        for o in range(1, NX):
            send(cs.at[dx(o)], cr.at[o - 1], c_s.at[o - 1], c_r.at[o - 1], (e, t, dx(o)))

    def chk2():
        for o in range(1, NX):
            got(cr.at[o - 1], c_s.at[o - 1], c_r.at[o - 1])
        cf[0] = cs[d] + cr[0] + cr[1] + cr[2]
        zr[t] = cf[0]
        for o in range(1, NT):
            send(cf.at[0], zr.at[t], z_s.at[o - 1], z_r.at[o - 1], (e, tz(o), d))

    def chk3():
        for o in range(1, NT):
            got(zr.at[tz(-o)], z_s.at[o - 1], z_r.at[o - 1])
        total = zr[0]
        for i in range(1, NT):
            total = total + zr[i]
        cf[1] = total
        cc[0] = total
        for j in range(1, n_exp):
            send(cf.at[1], cc.at[j], cc_s.at[j - 1], cc_r.at[j - 1], (source(j), t, d))

    iota_s = lax.broadcasted_iota(jnp.int32, (toks, rows), 1).astype(F32)

    def chk4():
        iota_l = lax.broadcasted_iota(jnp.int32, (toks, toks), 1).astype(F32)
        col = [turned(ids[k : k + 1]) for k in range(2)]
        left = [(col[k] == iota_l).astype(F32) for k in range(2)]
        below = lax.broadcasted_iota(jnp.int32, (toks, toks), 1) < lax.broadcasted_iota(jnp.int32, (toks, toks), 0)
        before_col = jnp.dot(
            below.astype(F32).astype(BF16), (left[0] + left[1]).astype(BF16), preferred_element_type=F32
        )
        pos = [jnp.sum(left[k] * before_col, axis=1, keepdims=True) for k in range(2)]
        gates = gate_ref[...].astype(F32)
        gate_sum = gates[0:1] + gates[1:2]
        weight = [turned(gates[k : k + 1] / gate_sum) for k in range(2)]
        for j in range(1, n_exp):
            got(cc.at[j], cc_s.at[j - 1], cc_r.at[j - 1])
        diff = jnp.zeros((toks, 1), F32)
        for k in range(2):
            row = jnp.zeros((toks, rows), F32)
            place = pos[k]
            for j in range(n_exp):
                here = col[k] == expert_at(j).astype(F32)
                row = row + jnp.where(here, jnp.broadcast_to(cc[j], (toks, rows)), 0.0)
                place = place + jnp.where(here, float(CAP * j), 0.0)
            picked = jnp.where(iota_s == place, row, 0.0)
            diff = diff + weight[k] * jnp.sum(picked, axis=1, keepdims=True)
        residual = jnp.transpose(jnp.broadcast_to(diff, (toks, toks)))[0:1] * (1.0 / math.sqrt(D))
        aux_ref[toks : toks + 1, :] = residual
        score = jnp.broadcast_to(jnp.sum(residual * residual, axis=1, keepdims=True), (1, toks))
        es[...] = score
        for o in range(1, NX):
            send(es, er.at[d], es_s.at[o - 1], es_r.at[o - 1], (e, t, dx(o)))
        er[d] = score
        table = jnp.zeros((toks, toks), F32)
        for k in range(2):
            table = jnp.where(iota_l == float(k), col[k] * float(CAP) + pos[k], table)
            table = jnp.where(iota_l == float(2 + k), weight[k], table)
        aux_ref[0:toks, :] = table

    def al1():
        for o in range(1, NX):
            got(er.at[dx(-o)], es_s.at[o - 1], es_r.at[o - 1])
        score = er[0]
        for i in range(1, NX):
            score = score + er[i]
        gs[...] = score
        for o in range(1, n_exp):
            send(gs, gr.at[e], gs_s.at[o - 1], gs_r.at[o - 1], (ex(o), t, d))
        gr[e] = score

    def al2():
        for o in range(1, n_exp):
            got(gr.at[ex(n_exp - o)], gs_s.at[o - 1], gs_r.at[o - 1])
        score = gr[0]
        for i in range(1, n_exp):
            score = score + gr[i]
        aux_ref[toks + 1 : toks + 2, :] = score * (1.0 / (toks * n_exp * NX))

    CHECKS = {"chk": chk, "chk2": chk2, "chk3": chk3, "chk4": chk4, "al1": al1, "al2": al2}
    for step in SCATTER:
        scatter(*step)

    for j in range(1, n_exp):
        got(qbuf.at[expert_at(j)], q_s.at[j - 1], q_r.at[j - 1])

    for o in range(n_exp - 1):
        sent(sbuf.at[0], d_s.at[o], d_r.at[o])
        sent(cf.at[1], cc_s.at[o], cc_r.at[o])
        sent(bbuf.at[0], q_s.at[o], q_r.at[o])
        sent(gs, gs_s.at[o], gs_r.at[o])
    for o in range(NX - 1):
        sent(cs.at[0], c_s.at[o], c_r.at[o])
        sent(es, es_s.at[o], es_r.at[o])
    for o in range(NT - 1):
        sent(cf.at[0], z_s.at[o], z_r.at[o])
    for ref, n in used:
        sent(ref, m_s.at[n], m_r.at[n])


def combine(back_ref, aux_ref, out_ref, res_ref, alarm_ref):
    n_exp, cap, cols = back_ref.shape
    toks = out_ref.shape[0]
    rows = n_exp * cap
    back = back_ref[...].astype(F32).reshape(rows, cols).astype(BF16)
    iota_s = lax.broadcasted_iota(jnp.int32, (toks, rows), 1).astype(F32)
    total = jnp.zeros((toks, cols), F32)
    for k in range(2):
        sel = (iota_s == aux_ref[0:toks, k : k + 1]).astype(F32).astype(BF16)
        total = total + aux_ref[0:toks, 2 + k : 3 + k] * jnp.dot(sel, back, preferred_element_type=F32)
    out_ref[...] = total
    res_ref[...] = aux_ref[toks : toks + 1, :]
    alarm_ref[...] = aux_ref[toks + 1 : toks + 2, 0:1]


def body(tokens, expert_ids, gate_fixed, w_gate, w_up, w_down, down_check):
    n_exp = lax.axis_size("expert")
    toks, cols = tokens.shape
    ff = w_gate.shape[2]
    rows = n_exp * CAP
    na = rows * 3 // 5
    nb = rows - na
    dma = lambda *s: pltpu.SemaphoreType.DMA(s)
    both = lambda *s: [dma(*s), dma(*s)]
    vm = pltpu.VMEM
    scratch = [
        vm((NT, ff, cols), BF16), vm((NT, ff, cols), BF16), vm((NT, ff, cols), BF16),
        vm((NT, NX, rows, cols), BF16), vm((NT, NX, rows, cols), BF16),
        vm((NX, na, ff), F32), vm((NX, na, ff), F32), vm((NX * nb, ff), F32), vm((NX * nb, ff), F32),
        vm((NX, rows, ff), BF16), vm((rows, cols), F32),
        vm((n_exp, CAP, cols), BF16), vm((n_exp, CAP, cols), BF16), vm((n_exp, CAP, cols), BF16),
        vm((NT, 2, na // 2, cols), BF16), vm((NT, 2, na, cols), BF16),
        vm((2, na // 2, cols), BF16), vm((3, 2, na, cols), BF16),
        vm((2, NX, nb // 2, cols), BF16), vm((3, 2, NX, nb, cols), BF16),
        vm((2, nb // 2, cols), BF16), vm((2, nb, cols), BF16),
        vm((NX, rows, min(cols, 128)), F32),
        vm((NX, 1, rows), F32), vm((NX - 1, 1, rows), F32), vm((2, 1, rows), F32), vm((NT, 1, rows), F32),
        vm((n_exp, 1, rows), F32), vm((1, toks), F32), vm((NX, 1, toks), F32),
        vm((1, toks), F32), vm((n_exp, 1, toks), F32),
        dma(3, NT), *both(n_exp - 1), *both(MESSAGES),
        *both(NX - 1), *both(n_exp - 1), *both(n_exp - 1), *both(NT - 1), *both(NX - 1), *both(n_exp - 1),
    ]
    vmem = pl.BlockSpec(memory_space=pltpu.VMEM)
    hbm = pl.BlockSpec(memory_space=pl.ANY)
    back, aux = pl.pallas_call(
        functools.partial(kernel, n_exp),
        out_shape=(
            jax.ShapeDtypeStruct((n_exp, CAP, cols), BF16),
            jax.ShapeDtypeStruct((toks + 8, toks), F32),
        ),
        in_specs=[vmem, vmem, vmem, vmem, hbm, hbm, hbm],
        out_specs=(vmem, vmem),
        scratch_shapes=scratch,
        compiler_params=pltpu.CompilerParams(
            collective_id=0, has_side_effects=True, vmem_limit_bytes=66_000_000
        ),
    )(
        tokens, expert_ids.T, gate_fixed.T, down_check,
        w_gate[0].T, w_up[0].T, w_down[0],
    )
    mix, residual, alarm = pl.pallas_call(
        combine,
        out_shape=(
            jax.ShapeDtypeStruct((toks, cols), F32),
            jax.ShapeDtypeStruct((1, toks), F32),
            jax.ShapeDtypeStruct((1, 1), F32),
        ),
        in_specs=[vmem, vmem],
        out_specs=(vmem, vmem, vmem),
    )(back, aux)
    return mix, residual.reshape(toks), alarm.reshape(())


def solution(mesh):
    return jax.shard_map(
        body,
        mesh=mesh,
        in_specs=(
            P(("expert", "dp"), "tensor"),
            P(("expert", "dp"), None),
            P(("expert", "dp"), None),
            P("expert", None, ("tensor", "dp")),
            P("expert", None, ("tensor", "dp")),
            P("expert", ("tensor", "dp"), None),
            P("expert", ("tensor", "dp")),
        ),
        out_specs=(P(("expert", "dp"), "tensor"), P(("expert", "dp")), P()),
        check_vma=False,
    )
```
